512 devices in a mesh: blk: 128 (over y, z, x_hi), col: 4 (over x_lo, core).
Axes of the slice: x: 4 (x_hi: 2, x_lo: 2; x = x_hi * 2 + x_lo), y: 8, z: 8, core: 2. Of those that a mesh axis runs over, the one named last changes fastest.
Arguments:
- start_panel: float32 [128, 262144], P('col', 'blk'), may hold values from -6 to 6
- tile_values: float32 [3072, 128, 128], P('blk'), may hold values from -0.3125 to 0.3125
- tile_rows: int32 [3072], P('blk'), may hold values from 0 to 2047, as said below
- tile_cols: int32 [3072], P('blk'), may hold values from 0 to 2047, as said below
- tile_counts: int32 [128], P('blk'), may hold values from 5 to 24, as said below
Outputs:
- ortho_panel: float32 [128, 262144], P('col', 'blk')
- gram_factor: float32 [128, 128], replicated
The draws below stay inside these ranges and needn't reach their ends.
Inputs may be any that keep to these rules, and one draw needn't show every extreme that they name: `tile_rows`: slot s has a row block among those of blk index s // 24, that is s // 24 * 16 up to s // 24 * 16 + 15. `tile_cols`: slot s has a column block among those of blk indices s // 24 + o for o from -2 to 2, taken modulo the number of blk indices; slot j of each blk index with j < 5 takes o = j - 2. `tile_counts`: some blk index has all 24 slots live; every blk index has 5 or more.
All inputs are finite; a program needn't handle non-finite values.
Results may differ from the reference program's by a relative error of at most 0.0003.
Values sent between devices are 32-bit elements; how exact they have to be, the bound alone decides.
No kernel may reach another device: no remote copies, remote signals or barrier semaphores. Data moves between devices by JAX's collectives and lax.ppermute only.
A program may use at most 64 MiB of HBM per device.

```python
import jax
import jax.numpy as jnp
from jax import lax

BS = 128
K = 128
RB_DEV = 16
TILE_CAP = 24
REACH = 2
DEGREE = 4
NB = 2048
NV = 262144
TILES = 3072
N_BLK = 128


def draw_tile_rows(key, part):
    owner = jnp.arange(TILES, dtype=jnp.int32) // TILE_CAP
    inside = jax.random.randint(key, (TILES,), 0, RB_DEV, dtype=jnp.int32)
    return owner * RB_DEV + inside


def draw_tile_cols(key, part):
    first, second = jax.random.split(key)
    slot_index = jnp.arange(TILES, dtype=jnp.int32)
    owner = slot_index // TILE_CAP
    within = slot_index % TILE_CAP
    random_offset = jax.random.randint(first, (TILES,), -REACH, REACH + 1, dtype=jnp.int32)
    offset = jnp.where(within < 2 * REACH + 1, within - REACH, random_offset)
    inside = jax.random.randint(second, (TILES,), 0, RB_DEV, dtype=jnp.int32)
    return (owner + offset + N_BLK) % N_BLK * RB_DEV + inside


def draw_tile_counts(key, part):
    first, second, third = jax.random.split(key, 3)
    lowest = 2 * REACH + 1
    highest = max(lowest, TILE_CAP // 2)
    base = jax.random.randint(first, (N_BLK,), lowest, highest + 1, dtype=jnp.int32)
    heavy = jax.random.randint(second, (N_BLK,), 0, 8, dtype=jnp.int32) == 0
    chosen = jax.random.randint(third, (), 0, N_BLK, dtype=jnp.int32)
    heavy = heavy | (jnp.arange(N_BLK, dtype=jnp.int32) == chosen)
    return jnp.where(heavy, jnp.int32(TILE_CAP), base)


def levels(rng, dims, cuts, smallest, top_value):
    gain, own = 1.0, jax.random.fold_in(rng, 6)
    for position, shards_of in cuts:
        draws = jnp.exp(jax.random.uniform(jax.random.fold_in(own, position), (shards_of,), jnp.float32, smallest / len(cuts), top_value / len(cuts)))
        gain = gain * jnp.repeat(draws, dims[position] // shards_of).reshape([-1 if axis == position else 1 for axis in range(len(dims))])
    return gain


def bell_draw(rng, dims, width, bound, cuts=(), kind=jnp.bfloat16):
    array = jax.random.normal(rng, dims, jnp.float32) * width
    if len(cuts) > 0:
        array = levels(rng, dims, cuts, -0.22, 0.18) * array
    return jnp.clip(array, min=-bound, max=bound).astype(kind)


def setup_inputs(seed: int = 0) -> dict:
    key_list = jax.random.split(jax.random.key(seed), 6)
    return {
        "start_panel": bell_draw(key_list[0], (K, NV), 1.0, 6.0, ((0, 4), (1, 128)), jnp.float32),
        "tile_values": bell_draw(key_list[1], (TILES, BS, BS), (3 * BS) ** -0.5, 0.3125, ((0, 128),), jnp.float32),
        "tile_rows": draw_tile_rows(jax.random.fold_in(key_list[5], 71), 0),
        "tile_cols": draw_tile_cols(jax.random.fold_in(key_list[5], 71), 0),
        "tile_counts": draw_tile_counts(jax.random.fold_in(key_list[5], 71), 0),
    }


def apply_graph(panel, tile_values, tile_rows, tile_cols, tile_counts):
    blocks = panel.reshape(K, NB, BS)
    values = tile_values.reshape(N_BLK, TILE_CAP, BS, BS)
    rows = tile_rows.reshape(N_BLK, TILE_CAP)
    cols = tile_cols.reshape(N_BLK, TILE_CAP)
    slots = jnp.arange(TILE_CAP, dtype=jnp.int32)

    def step(total, item):
        vals, rws, cls, count = item
        live = slots < count
        piece = blocks[:, cls, :]
        contrib = jnp.einsum('ktb,tab->kta', piece, vals, precision=lax.Precision.HIGHEST)
        contrib = jnp.where(live[None, :, None], contrib, jnp.zeros_like(contrib))
        total = total.at[:, rws, :].add(contrib)
        return (total, None)
    start = jnp.zeros((K, NB, BS), jnp.float32).astype(panel.dtype)
    total, unused = lax.scan(step, start, (values, rows, cols, tile_counts))
    return total.reshape(K, NV)

def reference(start_panel, tile_values, tile_rows, tile_cols, tile_counts):
    previous = start_panel
    current = apply_graph(start_panel, tile_values, tile_rows, tile_cols, tile_counts)
    for step in range(DEGREE - 1):
        upcoming = 2.0 * apply_graph(current, tile_values, tile_rows, tile_cols, tile_counts) - previous
        previous, current = (current, upcoming)
    gram = jnp.dot(current, current.T, precision=lax.Precision.HIGHEST)
    factor = jnp.linalg.cholesky(gram)
    scale = jnp.sqrt(jnp.asarray(NV, jnp.float32)).astype(current.dtype)
    solved = lax.linalg.triangular_solve(factor, current, left_side=True, lower=True)
    return (solved * scale, factor / scale)
```

```python
import functools

import jax
import jax.numpy as jnp
from jax import lax
from jax.experimental import pallas as pl
from jax.experimental.pallas import tpu as pltpu
from jax.sharding import Mesh
from jax.sharding import PartitionSpec as P

BS = 128
K = 128
RB_DEV = 16
TILE_CAP = 24
DEGREE = 4
COLS = 16
HALF = 2 * RB_DEV
UNROLL = 4
GROUP = ("xh", "xl", "core")
COL = ("xl", "core")
VMEM = pl.BlockSpec(memory_space=pltpu.VMEM)
SMEM = pl.BlockSpec(memory_space=pltpu.SMEM)
INTERPRET = False


def split_bf16(value):
    high = value.astype(jnp.bfloat16)
    low = (value - high.astype(jnp.float32)).astype(jnp.bfloat16)
    return high, low


def call(kernel, out_shape, operands, specs, scratch=(), flops=0, moved=0):
    outs = jax.tree.map(lambda s: VMEM, out_shape)
    return pl.pallas_call(
        kernel,
        out_shape=out_shape,
        in_specs=specs,
        out_specs=outs,
        scratch_shapes=list(scratch),
        compiler_params=pltpu.CompilerParams(vmem_limit_bytes=24 << 20),
        cost_estimate=pl.CostEstimate(flops=flops, bytes_accessed=moved, transcendentals=0),
        interpret=INTERPRET,
    )(*operands)


def split_kernel(*refs):
    *pieces, out_ref = refs
    base = 0
    for piece in pieces:
        def body(slot, carry, piece=piece, base=base):
            high, low = split_bf16(piece[slot])
            out_ref[base + slot, 0] = high
            out_ref[base + slot, 1] = low
            return carry

        lax.fori_loop(0, piece.shape[0], body, 0, unroll=2)
        base += piece.shape[0]


def split_tiles(pieces):
    count = sum(piece.shape[0] for piece in pieces)
    return call(
        split_kernel,
        jax.ShapeDtypeStruct((count, 2, BS, BS), jnp.bfloat16),
        pieces,
        [VMEM] * len(pieces),
        moved=count * BS * BS * 8,
    )


def dot_t(left, right, precision=None):
    return lax.dot_general(
        left,
        right,
        (((1,), (1,)), ((), ())),
        preferred_element_type=jnp.float32,
        precision=precision,
    )


def step_kernel(first, last, *refs):
    if first:
        table, low_ref, mid_ref, high_ref, own_ref, other_ref, out_ref, window, total = refs
        prev_ref = None
    else:
        table, low_ref, mid_ref, high_ref, prev_ref, own_ref, other_ref, out_ref, window, total = refs
    for piece, ref in enumerate((low_ref, mid_ref, high_ref)):
        def fill(block, carry, piece=piece, ref=ref):
            high, low = split_bf16(ref[block])
            window[piece * HALF + block, 0:COLS] = high
            window[piece * HALF + block, COLS : 2 * COLS] = low
            return carry

        lax.fori_loop(0, HALF, fill, 0, unroll=8)
    total[...] = jnp.zeros_like(total)
    for which, tiles in enumerate((own_ref, other_ref)):
        base = which * 3 * TILE_CAP
        live = table[6 * TILE_CAP + which]

        def body(group, carry, base=base, tiles=tiles, live=live):
            terms = []
            for inner in range(UNROLL):
                slot = group * UNROLL + inner
                column = table[base + TILE_CAP + slot]
                place = table[base + 2 * TILE_CAP + slot]
                both = window[column]
                wide = dot_t(both, tiles[place, 0])
                narrow = dot_t(both[:COLS], tiles[place, 1])
                term = wide[:COLS] + (wide[COLS:] + narrow)
                terms.append(jnp.where(slot < live, term, jnp.zeros_like(term)))
            for inner in range(UNROLL):
                row = table[base + group * UNROLL + inner]
                total[row] = total[row] + terms[inner]
            return carry

        lax.fori_loop(0, (live + UNROLL - 1) // UNROLL, body, 0)
    swap = table[6 * TILE_CAP + 2] if last else 0

    def finish(block, carry):
        source = block ^ swap if last else block
        value = total[source]
        if prev_ref is not None:
            value = 2.0 * value - prev_ref[source]
        out_ref[block] = value
        return carry

    lax.fori_loop(0, HALF, finish, 0, unroll=8)


def graph_step(table, parts, prev, own_tiles, other_tiles, last):
    first = prev is None
    operands = [table, *parts] + ([] if first else [prev]) + [own_tiles, other_tiles]
    return call(
        functools.partial(step_kernel, first, last),
        jax.ShapeDtypeStruct((HALF, COLS, BS), jnp.float32),
        operands,
        [SMEM] + [VMEM] * (len(operands) - 1),
        scratch=[
            pltpu.VMEM((3 * HALF, 2 * COLS, BS), jnp.bfloat16),
            pltpu.VMEM((HALF, COLS, BS), jnp.float32),
        ],
        flops=2 * TILE_CAP * 6 * COLS * BS * BS,
        moved=8 << 20,
    )


def gram_kernel(parts_ref, all_ref, gram_ref):
    for half in range(2):
        for c in range(4):
            for block in range(4):
                row = (2 * c + half) * COLS
                all_ref[row : row + COLS, block * BS : (block + 1) * BS] = parts_ref[
                    half * 4 + c, block
                ]
    value = all_ref[...]
    gram_ref[...] = dot_t(value, value, precision=lax.Precision.HIGHEST)


def apply_kernel(inverse_ref, all_ref, out_ref):
    out_ref[...] = lax.dot_general(
        inverse_ref[...],
        all_ref[...],
        (((1,), (0,)), ((), ())),
        preferred_element_type=jnp.float32,
        precision=lax.Precision.HIGHEST,
    )


def exchange(value, axis):
    return lax.ppermute(value, axis, [(0, 1), (1, 0)])


def to_all(value, axis):
    return lax.all_to_all(value, axis, 0, 0, tiled=True)


def filtered_basis(start_panel, tile_values, tile_rows, tile_cols, tile_counts):
    q = lax.axis_index("q")
    count_q = lax.axis_size("q")
    xh = lax.axis_index("xh")
    c = lax.axis_index("xl") * 2 + lax.axis_index("core")
    quarter = TILE_CAP // 4

    halves = start_panel.reshape(2, COLS, RB_DEV, BS)
    mine = lax.dynamic_index_in_dim(halves, xh, 0, keepdims=False).transpose(1, 0, 2)
    given = lax.dynamic_index_in_dim(halves, 1 - xh, 0, keepdims=False).transpose(1, 0, 2)
    notes = jnp.concatenate(
        [
            tile_rows.astype(jnp.float32)[None],
            tile_cols.astype(jnp.float32)[None],
            jnp.broadcast_to(tile_counts.astype(jnp.float32)[None], (1, TILE_CAP)),
        ],
        axis=0,
    )
    notes = jnp.pad(notes, ((0, COLS - 3), (0, BS - TILE_CAP)))
    got = exchange(jnp.concatenate([given, notes[None]], axis=0), "xh")
    panel = jnp.concatenate([mine, got[:RB_DEV]], axis=0)
    other = jnp.round(got[RB_DEV, :3, :TILE_CAP]).astype(jnp.int32)

    piece = lax.dynamic_slice_in_dim(tile_values, c * quarter, quarter, 0)
    first = lax.ppermute(piece, ("xh", "xl"), [(i, 3 - i) for i in range(4)])
    second = exchange(first, "xl")
    pair = jnp.concatenate([first, second], axis=0)
    far = exchange(pair, "core")
    own_tiles = split_tiles([tile_values])
    other_tiles = split_tiles([pair, far])

    slots = jnp.arange(TILE_CAP, dtype=jnp.int32)

    def window_place(cols):
        owner = cols // RB_DEV
        step = (owner // 2 - q + 1 + count_q) % count_q
        place = step * HALF + ((owner % 2) ^ xh) * RB_DEV + cols % RB_DEV
        return jnp.clip(place, 0, 3 * HALF - 1)

    def row_place(rows, base):
        return jnp.clip(rows % RB_DEV, 0, RB_DEV - 1) + base

    order = (slots // quarter) ^ c
    order = (order % 2) * 2 + 1 - order // 2
    table = jnp.concatenate(
        [
            row_place(tile_rows, 0),
            window_place(tile_cols),
            slots,
            row_place(other[0], RB_DEV),
            window_place(other[1]),
            order * quarter + slots % quarter,
            tile_counts,
            other[2, :1],
            (xh * RB_DEV)[None],
        ]
    )

    up = [(i, (i + 1) % count_q) for i in range(count_q)]
    down = [(i, (i - 1) % count_q) for i in range(count_q)]
    previous, current = None, panel
    for step in range(DEGREE):
        lower = lax.ppermute(current, "q", up)
        higher = lax.ppermute(current, "q", down)
        upcoming = graph_step(
            table, (lower, current, higher), previous, own_tiles, other_tiles, step == DEGREE - 1
        )
        previous, current = current, upcoming

    parts = to_all(current.reshape(8, 4, COLS, BS), GROUP)
    everything, gram = call(
        gram_kernel,
        (
            jax.ShapeDtypeStruct((K, 4 * BS), jnp.float32),
            jax.ShapeDtypeStruct((K, K), jnp.float32),
        ),
        [parts],
        [VMEM],
        flops=2 * K * K * 4 * BS * 6,
        moved=1 << 20,
    )
    rows = K // count_q if K >= count_q else 1
    spread = to_all(gram, "q").reshape(count_q, rows, K).sum(axis=0)
    spread = to_all(jnp.broadcast_to(spread[None], (8, rows, K)), GROUP).sum(axis=0)
    gram = to_all(jnp.broadcast_to(spread[None], (count_q, rows, K)), "q").reshape(K, K)

    factor = jnp.linalg.cholesky(gram)
    total_rows = start_panel.shape[1] * count_q * 2
    scale = jnp.sqrt(jnp.asarray(total_rows, jnp.float32))
    inverse = lax.linalg.triangular_solve(
        factor, jnp.eye(K, dtype=jnp.float32), left_side=True, lower=True
    )
    ortho = call(
        apply_kernel,
        jax.ShapeDtypeStruct((K, 4 * BS), jnp.float32),
        [inverse * scale, everything],
        [VMEM, VMEM],
        flops=2 * K * K * 4 * BS * 6,
        moved=1 << 20,
    )
    ortho = to_all(ortho.reshape(4, K // 4, 4 * BS), COL)
    ortho_panel = ortho.transpose(1, 0, 2).reshape(K // 4, 16 * BS)
    return (ortho_panel, factor / scale)


def solution(mesh):
    grid = Mesh(
        mesh.devices.reshape(mesh.devices.shape[0] // 2, 2, 2, 2), ("q", "xh", "xl", "core")
    )
    blk = ("q", "xh")
    in_specs = (P(COL, blk), P(blk, None, None), P(blk), P(blk), P(blk))
    out_specs = (P(COL, blk), P())
    return jax.shard_map(
        filtered_basis, mesh=grid, in_specs=in_specs, out_specs=out_specs, check_vma=False
    )
```

```python
import functools
import math

import jax
import jax.numpy as jnp
from jax import lax
from jax.experimental import pallas as pl
from jax.experimental.pallas import tpu as pltpu
from jax.sharding import Mesh
from jax.sharding import PartitionSpec as P

BS = 128
K = 128
RB_DEV = 16
TILE_CAP = 24
DEGREE = 4
COLS = 16
HALF = 2 * RB_DEV
UNROLL = 4
BLOCK = 32
FEW = 4
GROUP = ("xh", "xl", "core")
COL = ("xl", "core")
VMEM = pl.BlockSpec(memory_space=pltpu.VMEM)
SMEM = pl.BlockSpec(memory_space=pltpu.SMEM)
INTERPRET = False


def split_bf16(value):
    high = value.astype(jnp.bfloat16)
    low = (value - high.astype(jnp.float32)).astype(jnp.bfloat16)
    return high, low


def call(kernel, out_shape, operands, specs, scratch=(), flops=0, moved=0):
    outs = jax.tree.map(lambda s: VMEM, out_shape)
    return pl.pallas_call(
        kernel,
        out_shape=out_shape,
        in_specs=specs,
        out_specs=outs,
        scratch_shapes=list(scratch),
        compiler_params=pltpu.CompilerParams(vmem_limit_bytes=24 << 20),
        cost_estimate=pl.CostEstimate(flops=flops, bytes_accessed=moved, transcendentals=0),
        interpret=INTERPRET,
    )(*operands)


def split_kernel(*refs):
    *pieces, out_ref = refs
    base = 0
    for piece in pieces:
        def body(slot, carry, piece=piece, base=base):
            high, low = split_bf16(piece[slot])
            out_ref[base + slot, 0] = high
            out_ref[base + slot, 1] = low
            return carry

        lax.fori_loop(0, piece.shape[0], body, 0, unroll=2)
        base += piece.shape[0]


def split_tiles(pieces):
    count = sum(piece.shape[0] for piece in pieces)
    return call(
        split_kernel,
        jax.ShapeDtypeStruct((count, 2, BS, BS), jnp.bfloat16),
        pieces,
        [VMEM] * len(pieces),
        moved=count * BS * BS * 8,
    )


def dot_t(left, right, precision=None):
    return lax.dot_general(
        left,
        right,
        (((1,), (1,)), ((), ())),
        preferred_element_type=jnp.float32,
        precision=precision,
    )


def step_kernel(first, last, *refs):
    if first:
        table, low_ref, mid_ref, high_ref, own_ref, other_ref, out_ref, window, total = refs
        prev_ref = None
    else:
        table, low_ref, mid_ref, high_ref, prev_ref, own_ref, other_ref, out_ref, window, total = refs
    for piece, ref in enumerate((low_ref, mid_ref, high_ref)):
        def fill(block, carry, piece=piece, ref=ref):
            high, low = split_bf16(ref[block])
            window[piece * HALF + block, 0:COLS] = high
            window[piece * HALF + block, COLS : 2 * COLS] = low
            return carry

        lax.fori_loop(0, HALF, fill, 0, unroll=8)
    total[...] = jnp.zeros_like(total)
    for which, tiles in enumerate((own_ref, other_ref)):
        base = which * 3 * TILE_CAP
        live = table[6 * TILE_CAP + which]

        def body(group, carry, base=base, tiles=tiles, live=live):
            terms = []
            for inner in range(UNROLL):
                slot = group * UNROLL + inner
                column = table[base + TILE_CAP + slot]
                place = table[base + 2 * TILE_CAP + slot]
                both = window[column]
                wide = dot_t(both, tiles[place, 0])
                narrow = dot_t(both[:COLS], tiles[place, 1])
                term = wide[:COLS] + (wide[COLS:] + narrow)
                terms.append(jnp.where(slot < live, term, jnp.zeros_like(term)))
            for inner in range(UNROLL):
                row = table[base + group * UNROLL + inner]
                total[row] = total[row] + terms[inner]
            return carry

        lax.fori_loop(0, (live + UNROLL - 1) // UNROLL, body, 0)
    swap = table[6 * TILE_CAP + 2] if last else 0

    def finish(block, carry):
        source = block ^ swap if last else block
        value = total[source]
        if prev_ref is not None:
            value = 2.0 * value - prev_ref[source]
        out_ref[block] = value
        return carry

    lax.fori_loop(0, HALF, finish, 0, unroll=8)


def graph_step(table, parts, prev, own_tiles, other_tiles, last):
    first = prev is None
    operands = [table, *parts] + ([] if first else [prev]) + [own_tiles, other_tiles]
    return call(
        functools.partial(step_kernel, first, last),
        jax.ShapeDtypeStruct((HALF, COLS, BS), jnp.float32),
        operands,
        [SMEM] + [VMEM] * (len(operands) - 1),
        scratch=[
            pltpu.VMEM((3 * HALF, 2 * COLS, BS), jnp.bfloat16),
            pltpu.VMEM((HALF, COLS, BS), jnp.float32),
        ],
        flops=2 * TILE_CAP * 6 * COLS * BS * BS,
        moved=8 << 20,
    )


def gram_kernel(parts_ref, all_ref, gram_ref):
    for half in range(2):
        for c in range(4):
            for block in range(4):
                row = (2 * c + half) * COLS
                all_ref[row : row + COLS, block * BS : (block + 1) * BS] = parts_ref[
                    half * 4 + c, block
                ]
    value = all_ref[...]
    gram_ref[...] = dot_t(value, value, precision=lax.Precision.HIGHEST)


def dot_n(left, right):
    return lax.dot_general(
        left,
        right,
        (((1,), (0,)), ((), ())),
        preferred_element_type=jnp.float32,
        precision=lax.Precision.HIGHEST,
    )


def eliminate(value, size):
    shape = value.shape
    row = lax.broadcasted_iota(jnp.int32, shape, 0)
    for start in range(0, size, FEW):
        raw = [jnp.broadcast_to(value[:, start + b : start + b + 1], shape) for b in range(FEW)]
        lines = [jnp.broadcast_to(value[start + b : start + b + 1], shape) for b in range(FEW)]
        small = [
            [jnp.broadcast_to(raw[b][start + a : start + a + 1], shape) for b in range(a + 1)]
            for a in range(FEW)
        ]
        columns, ups = [], []
        for b in range(FEW):
            root = lax.rsqrt(small[b][b])
            for a in range(b + 1, FEW):
                small[a][b] = small[a][b] * root
            for a in range(b + 1, FEW):
                for c in range(b + 1, a + 1):
                    small[a][c] = small[a][c] - small[a][b] * small[c][b]
            column, up = raw[b], lines[b]
            for c in range(b):
                column = column - columns[c] * small[b][c]
                up = up - ups[c] * small[b][c]
            columns.append(column * root)
            ups.append(up * root)
        change = columns[0] * ups[0]
        for b in range(1, FEW):
            change = change + columns[b] * ups[b]
        value = jnp.where(row >= start + FEW, value - change, value)
        for b in range(FEW):
            value = jnp.where(row == start + b, ups[b], value)
    return value


def factor_kernel(scale, gram_ref, all_ref, factor_ref, ortho_ref, work):
    row = lax.broadcasted_iota(jnp.int32, (K, K), 0)
    lane = lax.broadcasted_iota(jnp.int32, (K, K), 1)
    work[:, :K] = gram_ref[...]
    work[:, K:] = (row == lane).astype(jnp.float32)
    small_row = lax.broadcasted_iota(jnp.int32, (BLOCK, K), 0)
    small_lane = lax.broadcasted_iota(jnp.int32, (BLOCK, K), 1)
    unit = (small_row + BLOCK == small_lane).astype(jnp.float32)
    for start in range(0, K, BLOCK):
        rows = slice(start, start + BLOCK)
        diagonal = work[rows, :K]
        if start:
            diagonal = pltpu.roll(diagonal, K - start, 1)
        done = eliminate(jnp.where(small_lane < BLOCK, diagonal, unit), BLOCK)
        inverse = pltpu.roll(done, K - BLOCK, 1)[:, :BLOCK]
        ups = dot_n(inverse, work[rows, :])
        work[rows, :] = ups
        below = start + BLOCK
        if below < K:
            change = dot_n(ups[:, :K].T, ups)
            work[below:, :] = work[below:, :] - change[below:]
    factor_ref[...] = (jnp.where(lane >= row, work[:, :K], 0.0) / scale).T
    ortho_ref[...] = dot_n(work[:, K:] * scale, all_ref[...])


def exchange(value, axis):
    return lax.ppermute(value, axis, [(0, 1), (1, 0)])


def to_all(value, axis):
    return lax.all_to_all(value, axis, 0, 0, tiled=True)


def filtered_basis(start_panel, tile_values, tile_rows, tile_cols, tile_counts):
    q = lax.axis_index("q")
    count_q = lax.axis_size("q")
    xh = lax.axis_index("xh")
    core = lax.axis_index("core")
    c = lax.axis_index("xl") * 2 + core
    quarter = TILE_CAP // 4

    halves = start_panel.reshape(2, COLS, RB_DEV, BS)
    mine = lax.dynamic_index_in_dim(halves, xh, 0, keepdims=False).transpose(1, 0, 2)
    given = lax.dynamic_index_in_dim(halves, 1 - xh, 0, keepdims=False).transpose(1, 0, 2)
    notes = jnp.concatenate(
        [
            tile_rows.astype(jnp.float32)[None],
            tile_cols.astype(jnp.float32)[None],
            jnp.broadcast_to(tile_counts.astype(jnp.float32)[None], (1, TILE_CAP)),
        ],
        axis=0,
    )
    notes = jnp.pad(notes, ((0, COLS - 3), (0, BS - TILE_CAP)))
    got = exchange(jnp.concatenate([given, notes[None]], axis=0), "xh")
    panel = jnp.concatenate([mine, got[:RB_DEV]], axis=0)
    other = jnp.round(got[RB_DEV, :3, :TILE_CAP]).astype(jnp.int32)

    piece = lax.dynamic_slice_in_dim(tile_values, c * quarter, quarter, 0)
    first = lax.ppermute(piece, ("xh", "xl"), [(i, 3 - i) for i in range(4)])
    second = exchange(first, "xl")
    pair = jnp.concatenate([first, second], axis=0)
    far = exchange(pair, "core")
    own_tiles = split_tiles([tile_values])
    other_tiles = split_tiles([pair, far])

    slots = jnp.arange(TILE_CAP, dtype=jnp.int32)

    def window_place(cols):
        owner = cols // RB_DEV
        step = (owner // 2 - q + 1 + count_q) % count_q
        step = jnp.where(core == 1, 2 - step, step)
        place = step * HALF + ((owner % 2) ^ xh) * RB_DEV + cols % RB_DEV
        return jnp.clip(place, 0, 3 * HALF - 1)

    def row_place(rows, base):
        return jnp.clip(rows % RB_DEV, 0, RB_DEV - 1) + base

    order = (slots // quarter) ^ c
    order = (order % 2) * 2 + 1 - order // 2
    table = jnp.concatenate(
        [
            row_place(tile_rows, 0),
            window_place(tile_cols),
            slots,
            row_place(other[0], RB_DEV),
            window_place(other[1]),
            order * quarter + slots % quarter,
            tile_counts,
            other[2, :1],
            (xh * RB_DEV)[None],
        ]
    )

    def pairs(shift):
        return [
            (2 * i + k, 2 * ((i + (shift if k == 0 else -shift)) % count_q) + k)
            for i in range(count_q)
            for k in range(2)
        ]

    previous, current = None, panel
    for step in range(DEGREE):
        lower = lax.ppermute(current, ("q", "core"), pairs(1))
        higher = lax.ppermute(current, ("q", "core"), pairs(-1))
        upcoming = graph_step(
            table, (lower, current, higher), previous, own_tiles, other_tiles, step == DEGREE - 1
        )
        previous, current = current, upcoming

    parts = to_all(current.reshape(8, 4, COLS, BS), GROUP)
    everything, gram = call(
        gram_kernel,
        (
            jax.ShapeDtypeStruct((K, 4 * BS), jnp.float32),
            jax.ShapeDtypeStruct((K, K), jnp.float32),
        ),
        [parts],
        [VMEM],
        flops=2 * K * K * 4 * BS * 6,
        moved=1 << 20,
    )
    rows = K // count_q if K >= count_q else 1
    spread = to_all(gram, "q").reshape(count_q, rows, K).sum(axis=0)
    spread = to_all(jnp.broadcast_to(spread[None], (8, rows, K)), GROUP).sum(axis=0)
    gram = to_all(jnp.broadcast_to(spread[None], (count_q, rows, K)), "q").reshape(K, K)

    total_rows = start_panel.shape[1] * count_q * 2
    factor, ortho = call(
        functools.partial(factor_kernel, math.sqrt(total_rows)),
        (
            jax.ShapeDtypeStruct((K, K), jnp.float32),
            jax.ShapeDtypeStruct((K, 4 * BS), jnp.float32),
        ),
        [gram, everything],
        [VMEM, VMEM],
        scratch=[pltpu.VMEM((K, 2 * K), jnp.float32)],
        flops=2 * K * K * 4 * BS * 6,
        moved=1 << 20,
    )
    ortho = to_all(ortho.reshape(4, K // 4, 4 * BS), COL)
    ortho_panel = ortho.transpose(1, 0, 2).reshape(K // 4, 16 * BS)
    return (ortho_panel, factor)


def solution(mesh):
    grid = Mesh(
        mesh.devices.reshape(mesh.devices.shape[0] // 2, 2, 2, 2), ("q", "xh", "xl", "core")
    )
    blk = ("q", "xh")
    in_specs = (P(COL, blk), P(blk, None, None), P(blk), P(blk), P(blk))
    out_specs = (P(COL, blk), P())
    return jax.shard_map(
        filtered_basis, mesh=grid, in_specs=in_specs, out_specs=out_specs, check_vma=False
    )
```

```python
import functools
import math

import jax
import jax.numpy as jnp
from jax import lax
from jax.experimental import pallas as pl
from jax.experimental.pallas import tpu as pltpu
from jax.sharding import Mesh
from jax.sharding import PartitionSpec as P

BS = 128
K = 128
RB_DEV = 16
TILE_CAP = 24
REACH = 2
DEGREE = 4
COLS = 16
HALF = 2 * RB_DEV
UNROLL = 4
BLOCK = 32
FEW = 4
GROUP = ("xh", "xl", "core")
COL = ("xl", "core")
VMEM = pl.BlockSpec(memory_space=pltpu.VMEM)
SMEM = pl.BlockSpec(memory_space=pltpu.SMEM)
INTERPRET = False


def split_bf16(value):
    high = value.astype(jnp.bfloat16)
    low = (value - high.astype(jnp.float32)).astype(jnp.bfloat16)
    return high, low


def call(kernel, out_shape, operands, specs, scratch=(), flops=0, moved=0):
    outs = jax.tree.map(lambda s: VMEM, out_shape)
    return pl.pallas_call(
        kernel,
        out_shape=out_shape,
        in_specs=specs,
        out_specs=outs,
        scratch_shapes=list(scratch),
        compiler_params=pltpu.CompilerParams(vmem_limit_bytes=24 << 20),
        cost_estimate=pl.CostEstimate(flops=flops, bytes_accessed=moved, transcendentals=0),
        interpret=INTERPRET,
    )(*operands)


def split_kernel(*refs):
    *pieces, out_ref = refs
    base = 0
    for piece in pieces:
        def body(slot, carry, piece=piece, base=base):
            high, low = split_bf16(piece[slot])
            out_ref[base + slot, 0] = high
            out_ref[base + slot, 1] = low
            return carry

        lax.fori_loop(0, piece.shape[0], body, 0, unroll=2)
        base += piece.shape[0]


def split_tiles(pieces):
    count = sum(piece.shape[0] for piece in pieces)
    return call(
        split_kernel,
        jax.ShapeDtypeStruct((count, 2, BS, BS), jnp.bfloat16),
        pieces,
        [VMEM] * len(pieces),
        moved=count * BS * BS * 8,
    )


def dot_t(left, right, precision=None):
    return lax.dot_general(
        left,
        right,
        (((1,), (1,)), ((), ())),
        preferred_element_type=jnp.float32,
        precision=precision,
    )


def step_kernel(last, *refs):
    table, low_ref, mid_ref, high_ref, prev_ref, own_ref, other_ref, out_ref, window, total = refs
    for piece, ref in enumerate((low_ref, mid_ref, high_ref)):
        def fill(block, carry, piece=piece, ref=ref):
            high, low = split_bf16(ref[block])
            window[piece * HALF + block, 0:COLS] = high
            window[piece * HALF + block, COLS : 2 * COLS] = low
            return carry

        lax.fori_loop(0, HALF, fill, 0, unroll=8)
    total[...] = jnp.zeros_like(total)
    for which, tiles in enumerate((own_ref, other_ref)):
        base = which * 3 * TILE_CAP
        live = table[6 * TILE_CAP + which]

        def body(group, carry, base=base, tiles=tiles, live=live):
            terms = []
            for inner in range(UNROLL):
                slot = group * UNROLL + inner
                column = table[base + TILE_CAP + slot]
                place = table[base + 2 * TILE_CAP + slot]
                both = window[column]
                wide = dot_t(both, tiles[place, 0])
                narrow = dot_t(both[:COLS], tiles[place, 1])
                term = wide[:COLS] + (wide[COLS:] + narrow)
                terms.append(jnp.where(slot < live, term, jnp.zeros_like(term)))
            for inner in range(UNROLL):
                row = table[base + group * UNROLL + inner]
                total[row] = total[row] + terms[inner]
            return carry

        lax.fori_loop(0, (live + UNROLL - 1) // UNROLL, body, 0)
    swap = table[6 * TILE_CAP + 2] if last else 0

    def finish(block, carry):
        source = block ^ swap if last else block
        out_ref[block] = 2.0 * total[source] - prev_ref[source]
        return carry

    lax.fori_loop(0, HALF, finish, 0, unroll=8)


def first_kernel(*refs):
    table, notes_ref, *pieces, tiles, mine_ref, given_ref, start_ref, window, total = refs
    wide_cols = 2 * COLS
    for piece, ref in enumerate(pieces):
        for block in range(RB_DEV):
            high, low = split_bf16(ref[:, block * BS : (block + 1) * BS])
            window[piece * RB_DEV + block, 0:wide_cols] = high
            window[piece * RB_DEV + block, wide_cols : 2 * wide_cols] = low
    total[...] = jnp.zeros_like(total)
    live = table[2 * TILE_CAP]
    upper = table[2 * TILE_CAP + 1] == 1

    def body(group, carry):
        terms = []
        for inner in range(UNROLL):
            slot = group * UNROLL + inner
            both = window[table[TILE_CAP + slot]]
            wide = dot_t(both, tiles[slot, 0])
            narrow = dot_t(both[:wide_cols], tiles[slot, 1])
            term = wide[:wide_cols] + (wide[wide_cols:] + narrow)
            terms.append(jnp.where(slot < live, term, jnp.zeros_like(term)))
        for inner in range(UNROLL):
            row = table[group * UNROLL + inner]
            total[row] = total[row] + terms[inner]
        return carry

    lax.fori_loop(0, (live + UNROLL - 1) // UNROLL, body, 0)
    for block in range(RB_DEV):
        value = total[block]
        mine_ref[block] = jnp.where(upper, value[COLS:], value[:COLS])
        given_ref[block] = jnp.where(upper, value[:COLS], value[COLS:])
        for half, ref in enumerate((pieces[0], pieces[3])):
            value = ref[:, block * BS : (block + 1) * BS]
            start_ref[half * RB_DEV + block] = jnp.where(upper, value[COLS:], value[:COLS])
    given_ref[RB_DEV] = notes_ref[...]


def graph_step(table, parts, prev, own_tiles, other_tiles, last):
    operands = [table, *parts, prev, own_tiles, other_tiles]
    return call(
        functools.partial(step_kernel, last),
        jax.ShapeDtypeStruct((HALF, COLS, BS), jnp.float32),
        operands,
        [SMEM] + [VMEM] * (len(operands) - 1),
        scratch=[
            pltpu.VMEM((3 * HALF, 2 * COLS, BS), jnp.bfloat16),
            pltpu.VMEM((HALF, COLS, BS), jnp.float32),
        ],
        flops=2 * TILE_CAP * 6 * COLS * BS * BS,
        moved=8 << 20,
    )


def gram_kernel(parts_ref, all_ref, gram_ref):
    for half in range(2):
        for c in range(4):
            for block in range(4):
                row = (2 * c + half) * COLS
                all_ref[row : row + COLS, block * BS : (block + 1) * BS] = parts_ref[
                    half * 4 + c, block
                ]
    value = all_ref[...]
    gram_ref[...] = dot_t(value, value, precision=lax.Precision.HIGHEST)


def dot_n(left, right):
    return lax.dot_general(
        left,
        right,
        (((1,), (0,)), ((), ())),
        preferred_element_type=jnp.float32,
        precision=lax.Precision.HIGHEST,
    )


def eliminate(value, size):
    shape = value.shape
    row = lax.broadcasted_iota(jnp.int32, shape, 0)
    for start in range(0, size, FEW):
        raw = [jnp.broadcast_to(value[:, start + b : start + b + 1], shape) for b in range(FEW)]
        lines = [jnp.broadcast_to(value[start + b : start + b + 1], shape) for b in range(FEW)]
        small = [
            [jnp.broadcast_to(raw[b][start + a : start + a + 1], shape) for b in range(a + 1)]
            for a in range(FEW)
        ]
        columns, ups = [], []
        for b in range(FEW):
            root = lax.rsqrt(small[b][b])
            for a in range(b + 1, FEW):
                small[a][b] = small[a][b] * root
            for a in range(b + 1, FEW):
                for c in range(b + 1, a + 1):
                    small[a][c] = small[a][c] - small[a][b] * small[c][b]
            column, up = raw[b], lines[b]
            for c in range(b):
                column = column - columns[c] * small[b][c]
                up = up - ups[c] * small[b][c]
            columns.append(column * root)
            ups.append(up * root)
        change = columns[0] * ups[0]
        for b in range(1, FEW):
            change = change + columns[b] * ups[b]
        value = jnp.where(row >= start + FEW, value - change, value)
        for b in range(FEW):
            value = jnp.where(row == start + b, ups[b], value)
    return value


def factor_kernel(scale, gram_ref, all_ref, factor_ref, ortho_ref, work):
    row = lax.broadcasted_iota(jnp.int32, (K, K), 0)
    lane = lax.broadcasted_iota(jnp.int32, (K, K), 1)
    work[:, :K] = gram_ref[...]
    work[:, K:] = (row == lane).astype(jnp.float32)
    small_row = lax.broadcasted_iota(jnp.int32, (BLOCK, K), 0)
    small_lane = lax.broadcasted_iota(jnp.int32, (BLOCK, K), 1)
    unit = (small_row + BLOCK == small_lane).astype(jnp.float32)
    for start in range(0, K, BLOCK):
        rows = slice(start, start + BLOCK)
        diagonal = work[rows, :K]
        if start:
            diagonal = pltpu.roll(diagonal, K - start, 1)
        done = eliminate(jnp.where(small_lane < BLOCK, diagonal, unit), BLOCK)
        inverse = pltpu.roll(done, K - BLOCK, 1)[:, :BLOCK]
        ups = dot_n(inverse, work[rows, :])
        work[rows, :] = ups
        below = start + BLOCK
        if below < K:
            change = dot_n(ups[:, :K].T, ups)
            work[below:, :] = work[below:, :] - change[below:]
    factor_ref[...] = (jnp.where(lane >= row, work[:, :K], 0.0) / scale).T
    ortho_ref[...] = dot_n(work[:, K:] * scale, all_ref[...])


def exchange(value, axis):
    return lax.ppermute(value, axis, [(0, 1), (1, 0)])


def to_all(value, axis):
    return lax.all_to_all(value, axis, 0, 0, tiled=True)


def filtered_basis(start_panel, tile_values, tile_rows, tile_cols, tile_counts):
    q = lax.axis_index("q")
    count_q = lax.axis_size("q")
    xh = lax.axis_index("xh")
    core = lax.axis_index("core")
    c = lax.axis_index("xl") * 2 + core
    quarter = TILE_CAP // 4

    def pairs(shift):
        return [
            (2 * i + k, 2 * ((i + (shift if k == 0 else -shift)) % count_q) + k)
            for i in range(count_q)
            for k in range(2)
        ]

    def halo(value):
        one = lax.ppermute(value, ("q", "core"), pairs(1))
        two = lax.ppermute(value, ("q", "core"), pairs(-1))
        return one, two

    count = 2 * count_q
    near = [(b, (b + 1 if b % 2 else b - 1) % count) for b in range(count)]
    diagonal = lax.ppermute(start_panel, ("q", "xh"), near)
    across = exchange(start_panel, "xh")
    one, two = halo(start_panel)
    piece = lax.dynamic_slice_in_dim(tile_values, c * quarter, quarter, 0)
    first = lax.ppermute(piece, ("xh", "xl"), [(i, 3 - i) for i in range(4)])
    second = exchange(first, "xl")
    pair = jnp.concatenate([first, second], axis=0)
    far = exchange(pair, "core")
    own_tiles = split_tiles([tile_values])
    other_tiles = split_tiles([pair, far])

    offset = (tile_cols // RB_DEV - 2 * q - xh + REACH + count) % count
    side = jnp.where(core == 1, 2 * REACH - offset, offset)
    place = jnp.where(offset % 2 == 1, jnp.where((offset == 3) == (xh == 0), 3, 4), 0)
    place = jnp.where(side == 0, 1, jnp.where(side == 4, 2, place))
    place = place * RB_DEV + tile_cols % RB_DEV
    own_table = jnp.concatenate([tile_rows % RB_DEV, place, tile_counts, xh[None]])
    notes = jnp.concatenate(
        [
            tile_rows.astype(jnp.float32)[None],
            tile_cols.astype(jnp.float32)[None],
            jnp.broadcast_to(tile_counts.astype(jnp.float32)[None], (1, TILE_CAP)),
        ],
        axis=0,
    )
    notes = jnp.pad(notes, ((0, COLS - 3), (0, BS - TILE_CAP)))
    half = jax.ShapeDtypeStruct((RB_DEV, COLS, BS), jnp.float32)
    mine, given, previous = call(
        first_kernel,
        (
            half,
            jax.ShapeDtypeStruct((RB_DEV + 1, COLS, BS), jnp.float32),
            jax.ShapeDtypeStruct((HALF, COLS, BS), jnp.float32),
        ),
        [own_table, notes, start_panel, one, two, across, diagonal, own_tiles],
        [SMEM] + [VMEM] * 7,
        scratch=[
            pltpu.VMEM((5 * RB_DEV, 4 * COLS, BS), jnp.bfloat16),
            pltpu.VMEM((RB_DEV, 2 * COLS, BS), jnp.float32),
        ],
        flops=2 * TILE_CAP * 6 * COLS * BS * BS,
        moved=4 << 20,
    )
    got = exchange(given, "xh")
    current = jnp.concatenate([mine, got[:RB_DEV]], axis=0)
    other = jnp.round(got[RB_DEV, :3, :TILE_CAP]).astype(jnp.int32)

    slots = jnp.arange(TILE_CAP, dtype=jnp.int32)

    def window_place(cols):
        owner = cols // RB_DEV
        step = (owner // 2 - q + 1 + count_q) % count_q
        step = jnp.where(core == 1, 2 - step, step)
        place = step * HALF + ((owner % 2) ^ xh) * RB_DEV + cols % RB_DEV
        return jnp.clip(place, 0, 3 * HALF - 1)

    def row_place(rows, base):
        return jnp.clip(rows % RB_DEV, 0, RB_DEV - 1) + base

    order = (slots // quarter) ^ c
    order = (order % 2) * 2 + 1 - order // 2
    table = jnp.concatenate(
        [
            row_place(tile_rows, 0),
            window_place(tile_cols),
            slots,
            row_place(other[0], RB_DEV),
            window_place(other[1]),
            order * quarter + slots % quarter,
            tile_counts,
            other[2, :1],
            (xh * RB_DEV)[None],
        ]
    )

    for step in range(1, DEGREE):
        lower, higher = halo(current)
        upcoming = graph_step(
            table, (lower, current, higher), previous, own_tiles, other_tiles, step == DEGREE - 1
        )
        previous, current = current, upcoming

    parts = to_all(current.reshape(8, 4, COLS, BS), GROUP)
    everything, gram = call(
        gram_kernel,
        (
            jax.ShapeDtypeStruct((K, 4 * BS), jnp.float32),
            jax.ShapeDtypeStruct((K, K), jnp.float32),
        ),
        [parts],
        [VMEM],
        flops=2 * K * K * 4 * BS * 6,
        moved=1 << 20,
    )
    rows = K // count_q if K >= count_q else 1
    spread = to_all(gram, "q").reshape(count_q, rows, K).sum(axis=0)
    spread = to_all(jnp.broadcast_to(spread[None], (8, rows, K)), GROUP).sum(axis=0)
    gram = to_all(jnp.broadcast_to(spread[None], (count_q, rows, K)), "q").reshape(K, K)

    total_rows = start_panel.shape[1] * count_q * 2
    factor, ortho = call(
        functools.partial(factor_kernel, math.sqrt(total_rows)),
        (
            jax.ShapeDtypeStruct((K, K), jnp.float32),
            jax.ShapeDtypeStruct((K, 4 * BS), jnp.float32),
        ),
        [gram, everything],
        [VMEM, VMEM],
        scratch=[pltpu.VMEM((K, 2 * K), jnp.float32)],
        flops=2 * K * K * 4 * BS * 6,
        moved=1 << 20,
    )
    ortho = to_all(ortho.reshape(4, K // 4, 4 * BS), COL)
    ortho_panel = ortho.transpose(1, 0, 2).reshape(K // 4, 16 * BS)
    return (ortho_panel, factor)


def solution(mesh):
    grid = Mesh(
        mesh.devices.reshape(mesh.devices.shape[0] // 2, 2, 2, 2), ("q", "xh", "xl", "core")
    )
    blk = ("q", "xh")
    in_specs = (P(COL, blk), P(blk, None, None), P(blk), P(blk), P(blk))
    out_specs = (P(COL, blk), P())
    return jax.shard_map(
        filtered_basis, mesh=grid, in_specs=in_specs, out_specs=out_specs, check_vma=False
    )
```

```python
import functools
import math

import jax
import jax.numpy as jnp
from jax import lax
from jax.experimental import pallas as pl
from jax.experimental.pallas import tpu as pltpu
from jax.sharding import Mesh
from jax.sharding import PartitionSpec as P

BS = 128
K = 128
RB_DEV = 16
TILE_CAP = 24
REACH = 2
DEGREE = 4
COLS = 16
HALF = 2 * RB_DEV
UNROLL = 4
BLOCK = 32
FEW = 4
GROUP = ("xh", "xl", "core")
COL = ("xl", "core")
VMEM = pl.BlockSpec(memory_space=pltpu.VMEM)
SMEM = pl.BlockSpec(memory_space=pltpu.SMEM)
INTERPRET = False


def split_bf16(value):
    high = value.astype(jnp.bfloat16)
    low = (value - high.astype(jnp.float32)).astype(jnp.bfloat16)
    return high, low


def call(kernel, out_shape, operands, specs, scratch=(), flops=0, moved=0):
    outs = jax.tree.map(lambda s: VMEM, out_shape)
    return pl.pallas_call(
        kernel,
        out_shape=out_shape,
        in_specs=specs,
        out_specs=outs,
        scratch_shapes=list(scratch),
        compiler_params=pltpu.CompilerParams(vmem_limit_bytes=24 << 20),
        cost_estimate=pl.CostEstimate(flops=flops, bytes_accessed=moved, transcendentals=0),
        interpret=INTERPRET,
    )(*operands)


def split_kernel(*refs):
    *pieces, out_ref = refs
    base = 0
    for piece in pieces:
        def body(slot, carry, piece=piece, base=base):
            high, low = split_bf16(piece[slot].T)
            out_ref[base + slot, 0] = high
            out_ref[base + slot, 1] = low
            return carry

        lax.fori_loop(0, piece.shape[0], body, 0, unroll=2)
        base += piece.shape[0]


def split_tiles(pieces):
    count = sum(piece.shape[0] for piece in pieces)
    return call(
        split_kernel,
        jax.ShapeDtypeStruct((count, 2, BS, BS), jnp.bfloat16),
        pieces,
        [VMEM] * len(pieces),
        moved=count * BS * BS * 8,
    )


def dot_t(left, right, precision=None):
    return lax.dot_general(
        left,
        right,
        (((1,), (1,)), ((), ())),
        preferred_element_type=jnp.float32,
        precision=precision,
    )


def list_kernel(count_q, ids, own_rows, own_cols, own_count, notes, lists):
    q, xh, c = ids[0], ids[1], ids[2]
    quarter = TILE_CAP // 4
    for which in range(6):
        lists[6 * TILE_CAP + which] = 0
    lists[6 * TILE_CAP + 6] = xh * RB_DEV

    def add(which, row, column, place):
        owner = column >> 4
        step = lax.rem((owner >> 1) - q + 1 + count_q, count_q)
        near = (step == 2) == ((q & 1) == 0)
        piece = jnp.where(step == 1, 0, jnp.where(near, 1, 2))
        local = ((owner & 1) ^ xh) * RB_DEV + (column & (RB_DEV - 1))
        target = piece * 2 + which
        fill = lists[6 * TILE_CAP + target]
        lists[target * TILE_CAP + fill] = row + HALF * local + HALF * HALF * place
        lists[6 * TILE_CAP + target] = fill + 1

    def own(slot, carry):
        add(0, own_rows[slot] & (RB_DEV - 1), own_cols[slot], slot)
        return carry

    def partner(slot, carry):
        row = (notes[0, slot].astype(jnp.int32) & (RB_DEV - 1)) + RB_DEV
        part = lax.div(slot, quarter)
        order = part ^ c
        order = (order & 1) * 2 + 1 - (order >> 1)
        place = order * quarter + slot - part * quarter
        add(1, row, notes[1, slot].astype(jnp.int32), place)
        return carry

    lax.fori_loop(0, own_count[0], own, 0)
    lax.fori_loop(0, notes[2, 0].astype(jnp.int32), partner, 0)


def part_kernel(piece, final, *refs):
    lists, source_ref, *middle, own_ref, other_ref, out_ref, window, total = refs

    def fill(block, carry):
        high, low = split_bf16(source_ref[block])
        window[block, 0:COLS] = high
        window[block, COLS : 2 * COLS] = low
        return carry

    lax.fori_loop(0, HALF, fill, 0, unroll=8)
    if piece == 0:
        total[...] = jnp.zeros_like(total)
    else:
        total[...] = middle[0][...]
    for which, tiles in enumerate((own_ref, other_ref)):
        base = (piece * 2 + which) * TILE_CAP
        live = lists[6 * TILE_CAP + piece * 2 + which]

        def body(group, carry, base=base, tiles=tiles, live=live):
            terms, rows = [], []
            for inner in range(UNROLL):
                slot = group * UNROLL + inner
                entry = jnp.where(slot < live, lists[base + slot], 0)
                both = window[(entry // HALF) % HALF]
                place = entry // (HALF * HALF)
                wide = dot_b(both, tiles[place, 0])
                narrow = dot_b(both[:COLS], tiles[place, 1])
                term = wide[:COLS] + (wide[COLS:] + narrow)
                terms.append(jnp.where(slot < live, term, jnp.zeros_like(term)))
                rows.append(entry % HALF)
            for inner in range(UNROLL):
                total[rows[inner]] = total[rows[inner]] + terms[inner]
            return carry

        lax.fori_loop(0, (live + UNROLL - 1) // UNROLL, body, 0)
    if piece < 2:
        out_ref[...] = total[...]
        return
    prev_ref = middle[1]
    swap = lists[6 * TILE_CAP + 6] if final else 0

    def finish(block, carry):
        source = block ^ swap if final else block
        out_ref[block] = 2.0 * total[source] - prev_ref[source]
        return carry

    lax.fori_loop(0, HALF, finish, 0, unroll=8)


def dot_b(left, right):
    return lax.dot_general(
        left, right, (((1,), (0,)), ((), ())), preferred_element_type=jnp.float32
    )


def first_kernel(count_b, *refs):
    ids, rows, cols, count, notes_ref, *refs = refs
    *pieces, tiles, mine_ref, given_ref, start_ref, window, total = refs
    q, xh = ids[0], ids[1]

    def place_of(column):
        offset = lax.rem((column >> 4) - 2 * q - xh + REACH + count_b, count_b)
        side = jnp.where((q & 1) == 0, 2 * REACH - offset, offset)
        place = jnp.where((offset & 1) == 1, jnp.where((offset == 3) == (xh == 0), 3, 4), 0)
        place = jnp.where(side == 0, 1, jnp.where(side == 4, 2, place))
        return place * RB_DEV + (column & (RB_DEV - 1))

    wide_cols = 2 * COLS
    for piece, ref in enumerate(pieces):
        for block in range(RB_DEV):
            high, low = split_bf16(ref[:, block * BS : (block + 1) * BS])
            window[piece * RB_DEV + block, 0:wide_cols] = high
            window[piece * RB_DEV + block, wide_cols : 2 * wide_cols] = low
    total[...] = jnp.zeros_like(total)
    live = count[0]
    upper = xh == 1

    def body(group, carry):
        terms = []
        for inner in range(UNROLL):
            slot = group * UNROLL + inner
            both = window[place_of(cols[slot])]
            high, low = split_bf16(tiles[slot])
            wide = dot_t(both, high)
            narrow = dot_t(both[:wide_cols], low)
            term = wide[:wide_cols] + (wide[wide_cols:] + narrow)
            terms.append(jnp.where(slot < live, term, jnp.zeros_like(term)))
        for inner in range(UNROLL):
            row = rows[group * UNROLL + inner] & (RB_DEV - 1)
            total[row] = total[row] + terms[inner]
        return carry

    lax.fori_loop(0, (live + UNROLL - 1) // UNROLL, body, 0)
    for block in range(RB_DEV):
        value = total[block]
        mine_ref[block] = jnp.where(upper, value[COLS:], value[:COLS])
        given_ref[block] = jnp.where(upper, value[:COLS], value[COLS:])
        for half, ref in enumerate((pieces[0], pieces[3])):
            value = ref[:, block * BS : (block + 1) * BS]
            start_ref[half * RB_DEV + block] = jnp.where(upper, value[COLS:], value[:COLS])
    given_ref[RB_DEV] = notes_ref[...]


def graph_part(lists, piece, source, middle, own_tiles, other_tiles, final):
    operands = [lists, source, *middle, own_tiles, other_tiles]
    return call(
        functools.partial(part_kernel, piece, final),
        jax.ShapeDtypeStruct((HALF, COLS, BS), jnp.float32),
        operands,
        [SMEM] + [VMEM] * (len(operands) - 1),
        scratch=[
            pltpu.VMEM((HALF, 2 * COLS, BS), jnp.bfloat16),
            pltpu.VMEM((HALF, COLS, BS), jnp.float32),
        ],
        flops=2 * TILE_CAP * 2 * COLS * BS * BS,
        moved=4 << 20,
    )


def gram_kernel(parts_ref, all_ref, gram_ref):
    for half in range(2):
        for c in range(4):
            for block in range(4):
                row = (2 * c + half) * COLS
                all_ref[row : row + COLS, block * BS : (block + 1) * BS] = parts_ref[
                    half * 4 + c, block
                ]
    value = all_ref[...]
    gram_ref[...] = dot_t(value, value, precision=lax.Precision.HIGHEST)


def dot_n(left, right):
    return lax.dot_general(
        left,
        right,
        (((1,), (0,)), ((), ())),
        preferred_element_type=jnp.float32,
        precision=lax.Precision.HIGHEST,
    )


def eliminate(value, size):
    shape = value.shape
    row = lax.broadcasted_iota(jnp.int32, shape, 0)
    for start in range(0, size, FEW):
        raw = [jnp.broadcast_to(value[:, start + b : start + b + 1], shape) for b in range(FEW)]
        lines = [jnp.broadcast_to(value[start + b : start + b + 1], shape) for b in range(FEW)]
        small = [
            [jnp.broadcast_to(raw[b][start + a : start + a + 1], shape) for b in range(a + 1)]
            for a in range(FEW)
        ]
        columns, ups = [], []
        for b in range(FEW):
            root = lax.rsqrt(small[b][b])
            for a in range(b + 1, FEW):
                small[a][b] = small[a][b] * root
            for a in range(b + 1, FEW):
                for c in range(b + 1, a + 1):
                    small[a][c] = small[a][c] - small[a][b] * small[c][b]
            column, up = raw[b], lines[b]
            for c in range(b):
                column = column - columns[c] * small[b][c]
                up = up - ups[c] * small[b][c]
            columns.append(column * root)
            ups.append(up * root)
        change = columns[0] * ups[0]
        for b in range(1, FEW):
            change = change + columns[b] * ups[b]
        value = jnp.where(row >= start + FEW, value - change, value)
        for b in range(FEW):
            value = jnp.where(row == start + b, ups[b], value)
    return value


def factor_kernel(scale, place_ref, gram_ref, *refs):
    *slices, factor_ref, ortho_ref, work = refs
    row = lax.broadcasted_iota(jnp.int32, (K, K), 0)
    lane = lax.broadcasted_iota(jnp.int32, (K, K), 1)
    work[:, :K] = gram_ref[...]
    work[:, K:] = (row == lane).astype(jnp.float32)
    small_row = lax.broadcasted_iota(jnp.int32, (BLOCK, K), 0)
    small_lane = lax.broadcasted_iota(jnp.int32, (BLOCK, K), 1)
    unit = (small_row + BLOCK == small_lane).astype(jnp.float32)
    for start in range(0, K, BLOCK):
        rows = slice(start, start + BLOCK)
        diagonal = work[rows, :K]
        if start:
            diagonal = pltpu.roll(diagonal, K - start, 1)
        done = eliminate(jnp.where(small_lane < BLOCK, diagonal, unit), BLOCK)
        inverse = pltpu.roll(done, K - BLOCK, 1)[:, :BLOCK]
        ups = dot_n(inverse, work[rows, :])
        work[rows, :] = ups
        below = start + BLOCK
        if below < K:
            change = dot_n(ups[:, :K].T, ups)
            work[below:, :] = work[below:, :] - change[below:]
    factor_ref[...] = (jnp.where(lane >= row, work[:, :K], 0.0) / scale).T
    own = place_ref[0]
    count = K // 4
    inverse = work[pl.ds(pl.multiple_of(own * count, count), count), K:] * scale
    width = 4 * BS
    mine, second, pair = slices
    for other, value in (
        (0, mine[...]),
        (2, second[...]),
        (1, pair[:K]),
        (3, pair[K:]),
    ):
        start = pl.multiple_of((own ^ other) * width, width)
        ortho_ref[:, pl.ds(start, width)] = dot_n(inverse, value)


def exchange(value, axis):
    return lax.ppermute(value, axis, [(0, 1), (1, 0)])


def to_all(value, axis):
    return lax.all_to_all(value, axis, 0, 0, tiled=True)


def filtered_basis(start_panel, tile_values, tile_rows, tile_cols, tile_counts):
    q = lax.axis_index("q")
    count_q = lax.axis_size("q")
    xh = lax.axis_index("xh")
    core = lax.axis_index("core")
    c = lax.axis_index("xl") * 2 + core
    quarter = TILE_CAP // 4

    even = [(i, i ^ 1) for i in range(count_q)]
    odd = [(i, (i + 1 if i % 2 else i - 1) % count_q) for i in range(count_q)]

    def halo(value):
        one = lax.ppermute(value, "q", even)
        two = lax.ppermute(value, "q", odd)
        return one, two

    count = 2 * count_q
    near = [(b, (b + 1 if b % 2 else b - 1) % count) for b in range(count)]
    diagonal = lax.ppermute(start_panel, ("q", "xh"), near)
    across = exchange(start_panel, "xh")
    one, two = halo(start_panel)
    piece = lax.dynamic_slice_in_dim(tile_values, c * quarter, quarter, 0)
    first = lax.ppermute(piece, ("xh", "xl"), [(i, 3 - i) for i in range(4)])
    second = exchange(first, "xl")
    pair = jnp.concatenate([first, second], axis=0)
    far = exchange(pair, "core")
    own_tiles = split_tiles([tile_values])
    other_tiles = split_tiles([pair, far])

    ids = jnp.stack([q, xh, c])
    notes = jnp.concatenate(
        [
            tile_rows.astype(jnp.float32)[None],
            tile_cols.astype(jnp.float32)[None],
            jnp.broadcast_to(tile_counts.astype(jnp.float32)[None], (1, TILE_CAP)),
        ],
        axis=0,
    )
    notes = jnp.pad(notes, ((0, COLS - 3), (0, BS - TILE_CAP)))
    half = jax.ShapeDtypeStruct((RB_DEV, COLS, BS), jnp.float32)
    mine, given, previous = call(
        functools.partial(first_kernel, count),
        (
            half,
            jax.ShapeDtypeStruct((RB_DEV + 1, COLS, BS), jnp.float32),
            jax.ShapeDtypeStruct((HALF, COLS, BS), jnp.float32),
        ),
        [
            ids, tile_rows, tile_cols, tile_counts,
            notes, start_panel, one, two, across, diagonal, tile_values,
        ],
        [SMEM] * 4 + [VMEM] * 7,
        scratch=[
            pltpu.VMEM((5 * RB_DEV, 4 * COLS, BS), jnp.bfloat16),
            pltpu.VMEM((RB_DEV, 2 * COLS, BS), jnp.float32),
        ],
        flops=2 * TILE_CAP * 6 * COLS * BS * BS,
        moved=4 << 20,
    )
    got = exchange(given, "xh")
    current = jnp.concatenate([mine, got[:RB_DEV]], axis=0)
    lists = pl.pallas_call(
        functools.partial(list_kernel, count_q),
        out_shape=jax.ShapeDtypeStruct((6 * TILE_CAP + 7,), jnp.int32),
        in_specs=[SMEM] * 5,
        out_specs=SMEM,
        interpret=INTERPRET,
        name="lists",
    )(ids, tile_rows, tile_cols, tile_counts, got[RB_DEV, :3, :TILE_CAP])
    for step in range(1, DEGREE):
        one, two = halo(current)
        final = step == DEGREE - 1
        tiles = (own_tiles, other_tiles, final)
        part = graph_part(lists, 0, current, (), *tiles)
        part = graph_part(lists, 1, one, (part,), *tiles)
        upcoming = graph_part(lists, 2, two, (part, previous), *tiles)
        previous, current = current, upcoming

    parts = to_all(current.reshape(8, 4, COLS, BS), GROUP)
    everything, gram = call(
        gram_kernel,
        (
            jax.ShapeDtypeStruct((K, 4 * BS), jnp.float32),
            jax.ShapeDtypeStruct((K, K), jnp.float32),
        ),
        [parts],
        [VMEM],
        flops=2 * K * K * 4 * BS * 6,
        moved=1 << 20,
    )
    second = exchange(everything, "xl")
    far_slices = exchange(jnp.concatenate([everything, second], axis=0), "core")
    rows = K // count_q if K >= count_q else 1
    spread = to_all(gram, "q").reshape(count_q, rows, K).sum(axis=0)
    spread = to_all(jnp.broadcast_to(spread[None], (8, rows, K)), GROUP).sum(axis=0)
    gram = to_all(jnp.broadcast_to(spread[None], (count_q, rows, K)), "q").reshape(K, K)

    total_rows = start_panel.shape[1] * count_q * 2
    factor, ortho_panel = call(
        functools.partial(factor_kernel, math.sqrt(total_rows)),
        (
            jax.ShapeDtypeStruct((K, K), jnp.float32),
            jax.ShapeDtypeStruct((K // 4, 16 * BS), jnp.float32),
        ),
        [c[None], gram, everything, second, far_slices],
        [SMEM] + [VMEM] * 4,
        scratch=[pltpu.VMEM((K, 2 * K), jnp.float32)],
        flops=2 * K * K * 4 * BS * 6,
        moved=1 << 20,
    )
    return (ortho_panel, factor)


def solution(mesh):
    grid = Mesh(
        mesh.devices.reshape(mesh.devices.shape[0] // 2, 2, 2, 2), ("q", "xh", "xl", "core")
    )
    blk = ("q", "xh")
    in_specs = (P(COL, blk), P(blk, None, None), P(blk), P(blk), P(blk))
    out_specs = (P(COL, blk), P())
    return jax.shard_map(
        filtered_basis, mesh=grid, in_specs=in_specs, out_specs=out_specs, check_vma=False
    )
```

```python
import functools
import math

import jax
import jax.numpy as jnp
from jax import lax
from jax.experimental import pallas as pl
from jax.experimental.pallas import tpu as pltpu
from jax.sharding import Mesh
from jax.sharding import PartitionSpec as P

BS = 128
K = 128
RB_DEV = 16
TILE_CAP = 24
REACH = 2
DEGREE = 4
COLS = 16
HALF = 2 * RB_DEV
UNROLL = 4
CHUNKS = 4
BLOCK = 32
FEW = 4
GROUP = ("xh", "xl", "core")
COL = ("xl", "core")
VMEM = pl.BlockSpec(memory_space=pltpu.VMEM)
SMEM = pl.BlockSpec(memory_space=pltpu.SMEM)
INTERPRET = False


def in_hbm(value):
    return value if INTERPRET else pltpu.with_memory_space_constraint(value, pltpu.MemorySpace.HBM)


def split_bf16(value):
    high = value.astype(jnp.bfloat16)
    low = (value - high.astype(jnp.float32)).astype(jnp.bfloat16)
    return high, low


def call(kernel, out_shape, operands, specs, scratch=(), flops=0, moved=0):
    outs = jax.tree.map(lambda s: VMEM, out_shape)
    return pl.pallas_call(
        kernel,
        out_shape=out_shape,
        in_specs=specs,
        out_specs=outs,
        scratch_shapes=list(scratch),
        compiler_params=pltpu.CompilerParams(vmem_limit_bytes=24 << 20),
        cost_estimate=pl.CostEstimate(flops=flops, bytes_accessed=moved, transcendentals=0),
        interpret=INTERPRET,
    )(*operands)


def sort_slots(ids, count_q, live, slot_of, lists):
    q, xh = ids[0], ids[1]

    def body(slot, fills):
        row, column, place = slot_of(slot)
        owner = column >> 4
        step = lax.rem((owner >> 1) - q + 1 + count_q, count_q)
        near = (step == 2) == ((q & 1) == 0)
        piece = jnp.where(step == 1, 0, jnp.where(near, 1, 2))
        local = ((owner & 1) ^ xh) * RB_DEV + (column & (RB_DEV - 1))
        fill = jnp.where(piece == 0, fills[0], jnp.where(piece == 1, fills[1], fills[2]))
        lists[piece * TILE_CAP + fill] = row + HALF * local + HALF * HALF * place
        return tuple(fills[k] + (piece == k).astype(jnp.int32) for k in range(3))

    zero = jnp.int32(0)
    fills = lax.fori_loop(0, live, body, (zero, zero, zero))
    for k in range(3):
        lists[3 * TILE_CAP + k] = fills[k]
    lists[3 * TILE_CAP + 3] = xh * RB_DEV


def split_into(value, out_ref, slot):
    high, low = split_bf16(value.T)
    out_ref[slot, 0] = high
    out_ref[slot, 1] = low


def own_kernel(count_q, ids, rows, cols, count, tiles, split_ref, piece_ref, lists, held, sems):
    chunk = TILE_CAP // CHUNKS
    copies = []
    for k in range(CHUNKS):
        part = pl.ds(k * chunk, chunk)
        copies.append(pltpu.make_async_copy(tiles.at[part], held.at[part], sems.at[k]))
        copies[-1].start()

    def slot_of(slot):
        return rows[slot] & (RB_DEV - 1), cols[slot], slot

    sort_slots(ids, count_q, count[0], slot_of, lists)
    for k in range(CHUNKS):
        copies[k].wait()

        def body(slot, carry):
            split_into(held[slot], split_ref, slot)
            return carry

        lax.fori_loop(k * chunk, (k + 1) * chunk, body, 0, unroll=2)
    quarter = TILE_CAP // 4
    for k in range(quarter):
        piece_ref[k] = held[ids[2] * quarter + k]


def other_kernel(count_q, ids, notes, pair, far, split_ref, lists):
    quarter = TILE_CAP // 4

    def slot_of(slot):
        row = (notes[0, slot].astype(jnp.int32) & (RB_DEV - 1)) + RB_DEV
        part = lax.div(slot, quarter)
        order = part ^ ids[2]
        order = (order & 1) * 2 + 1 - (order >> 1)
        return row, notes[1, slot].astype(jnp.int32), order * quarter + slot - part * quarter

    sort_slots(ids, count_q, notes[2, 0].astype(jnp.int32), slot_of, lists)
    for base, piece in ((0, pair), (2 * quarter, far)):
        def body(slot, carry, base=base, piece=piece):
            split_into(piece[slot], split_ref, base + slot)
            return carry

        lax.fori_loop(0, 2 * quarter, body, 0, unroll=2)


def dot_t(left, right, precision=None):
    return lax.dot_general(
        left,
        right,
        (((1,), (1,)), ((), ())),
        preferred_element_type=jnp.float32,
        precision=precision,
    )


def part_kernel(piece, final, *refs):
    own_list, other_list, source_ref, *middle, own_ref, other_ref, out_ref, window, total = refs

    def fill(block, carry):
        high, low = split_bf16(source_ref[block])
        window[block, 0:COLS] = high
        window[block, COLS : 2 * COLS] = low
        return carry

    lax.fori_loop(0, HALF, fill, 0, unroll=8)
    if piece == 0:
        total[...] = jnp.zeros_like(total)
    else:
        total[...] = middle[0][...]
    base = piece * TILE_CAP
    for lists, tiles in ((own_list, own_ref), (other_list, other_ref)):
        live = lists[3 * TILE_CAP + piece]

        def body(group, carry, lists=lists, tiles=tiles, live=live):
            terms, rows = [], []
            for inner in range(UNROLL):
                slot = group * UNROLL + inner
                entry = jnp.where(slot < live, lists[base + slot], 0)
                both = window[(entry // HALF) % HALF]
                place = entry // (HALF * HALF)
                wide = dot_b(both, tiles[place, 0])
                narrow = dot_b(both[:COLS], tiles[place, 1])
                term = wide[:COLS] + (wide[COLS:] + narrow)
                terms.append(jnp.where(slot < live, term, jnp.zeros_like(term)))
                rows.append(entry % HALF)
            for inner in range(UNROLL):
                total[rows[inner]] = total[rows[inner]] + terms[inner]
            return carry

        lax.fori_loop(0, (live + UNROLL - 1) // UNROLL, body, 0)
    if piece < 2:
        out_ref[...] = total[...]
        return
    prev_ref = middle[1]
    swap = own_list[3 * TILE_CAP + 3] if final else 0

    def finish(block, carry):
        source = block ^ swap if final else block
        out_ref[block] = 2.0 * total[source] - prev_ref[source]
        return carry

    lax.fori_loop(0, HALF, finish, 0, unroll=8)


def dot_b(left, right):
    return lax.dot_general(
        left, right, (((1,), (0,)), ((), ())), preferred_element_type=jnp.float32
    )


def first_kernel(count_b, *refs):
    ids, rows, cols, count, notes_ref, *refs = refs
    *pieces, tiles, mine_ref, given_ref, start_ref, window, total = refs
    q, xh = ids[0], ids[1]

    def place_of(column):
        offset = lax.rem((column >> 4) - 2 * q - xh + REACH + count_b, count_b)
        side = jnp.where((q & 1) == 0, 2 * REACH - offset, offset)
        place = jnp.where((offset & 1) == 1, jnp.where((offset == 3) == (xh == 0), 3, 4), 0)
        place = jnp.where(side == 0, 1, jnp.where(side == 4, 2, place))
        return place * RB_DEV + (column & (RB_DEV - 1))

    wide_cols = 2 * COLS
    for piece, ref in enumerate(pieces):
        for block in range(RB_DEV):
            high, low = split_bf16(ref[:, block * BS : (block + 1) * BS])
            window[piece * RB_DEV + block, 0:wide_cols] = high
            window[piece * RB_DEV + block, wide_cols : 2 * wide_cols] = low
    total[...] = jnp.zeros_like(total)
    live = count[0]
    upper = xh == 1

    def body(group, carry):
        terms = []
        for inner in range(UNROLL):
            slot = group * UNROLL + inner
            both = window[place_of(cols[slot])]
            wide = dot_b(both, tiles[slot, 0])
            narrow = dot_b(both[:wide_cols], tiles[slot, 1])
            term = wide[:wide_cols] + (wide[wide_cols:] + narrow)
            terms.append(jnp.where(slot < live, term, jnp.zeros_like(term)))
        for inner in range(UNROLL):
            row = rows[group * UNROLL + inner] & (RB_DEV - 1)
            total[row] = total[row] + terms[inner]
        return carry

    lax.fori_loop(0, (live + UNROLL - 1) // UNROLL, body, 0)
    for block in range(RB_DEV):
        value = total[block]
        mine_ref[block] = jnp.where(upper, value[COLS:], value[:COLS])
        given_ref[block] = jnp.where(upper, value[:COLS], value[COLS:])
        for half, ref in enumerate((pieces[0], pieces[3])):
            value = ref[:, block * BS : (block + 1) * BS]
            start_ref[half * RB_DEV + block] = jnp.where(upper, value[COLS:], value[:COLS])
    given_ref[RB_DEV] = notes_ref[...]


def graph_part(lists, piece, source, middle, own_tiles, other_tiles, final):
    operands = [*lists, source, *middle, own_tiles, other_tiles]
    return call(
        functools.partial(part_kernel, piece, final),
        jax.ShapeDtypeStruct((HALF, COLS, BS), jnp.float32),
        operands,
        [SMEM] * 2 + [VMEM] * (len(operands) - 2),
        scratch=[
            pltpu.VMEM((HALF, 2 * COLS, BS), jnp.bfloat16),
            pltpu.VMEM((HALF, COLS, BS), jnp.float32),
        ],
        flops=2 * TILE_CAP * 2 * COLS * BS * BS,
        moved=4 << 20,
    )


def gram_kernel(parts_ref, all_ref, gram_ref):
    for half in range(2):
        for c in range(4):
            for block in range(4):
                row = (2 * c + half) * COLS
                all_ref[row : row + COLS, block * BS : (block + 1) * BS] = parts_ref[
                    half * 4 + c, block
                ]
    value = all_ref[...]
    gram_ref[...] = dot_t(value, value, precision=lax.Precision.HIGHEST)


def dot_n(left, right):
    return lax.dot_general(
        left,
        right,
        (((1,), (0,)), ((), ())),
        preferred_element_type=jnp.float32,
        precision=lax.Precision.HIGHEST,
    )


def eliminate(value, size):
    shape = value.shape
    row = lax.broadcasted_iota(jnp.int32, shape, 0)
    for start in range(0, size, FEW):
        raw = [jnp.broadcast_to(value[:, start + b : start + b + 1], shape) for b in range(FEW)]
        lines = [jnp.broadcast_to(value[start + b : start + b + 1], shape) for b in range(FEW)]
        small = [
            [jnp.broadcast_to(raw[b][start + a : start + a + 1], shape) for b in range(a + 1)]
            for a in range(FEW)
        ]
        columns, ups = [], []
        for b in range(FEW):
            root = lax.rsqrt(small[b][b])
            for a in range(b + 1, FEW):
                small[a][b] = small[a][b] * root
            for a in range(b + 1, FEW):
                for c in range(b + 1, a + 1):
                    small[a][c] = small[a][c] - small[a][b] * small[c][b]
            column, up = raw[b], lines[b]
            for c in range(b):
                column = column - columns[c] * small[b][c]
                up = up - ups[c] * small[b][c]
            columns.append(column * root)
            ups.append(up * root)
        change = columns[0] * ups[0]
        for b in range(1, FEW):
            change = change + columns[b] * ups[b]
        value = jnp.where(row >= start + FEW, value - change, value)
        for b in range(FEW):
            value = jnp.where(row == start + b, ups[b], value)
    return value


def factor_kernel(scale, place_ref, gram_ref, *refs):
    *slices, factor_ref, ortho_ref, work = refs
    row = lax.broadcasted_iota(jnp.int32, (K, K), 0)
    lane = lax.broadcasted_iota(jnp.int32, (K, K), 1)
    work[:, :K] = gram_ref[...]
    work[:, K:] = (row == lane).astype(jnp.float32)
    small_row = lax.broadcasted_iota(jnp.int32, (BLOCK, K), 0)
    small_lane = lax.broadcasted_iota(jnp.int32, (BLOCK, K), 1)
    unit = (small_row + BLOCK == small_lane).astype(jnp.float32)
    for start in range(0, K, BLOCK):
        rows = slice(start, start + BLOCK)
        diagonal = work[rows, :K]
        if start:
            diagonal = pltpu.roll(diagonal, K - start, 1)
        done = eliminate(jnp.where(small_lane < BLOCK, diagonal, unit), BLOCK)
        inverse = pltpu.roll(done, K - BLOCK, 1)[:, :BLOCK]
        ups = dot_n(inverse, work[rows, :])
        work[rows, :] = ups
        below = start + BLOCK
        if below < K:
            change = dot_n(ups[:, :K].T, ups)
            work[below:, :] = work[below:, :] - change[below:]
    factor_ref[...] = (jnp.where(lane >= row, work[:, :K], 0.0) / scale).T
    own = place_ref[0]
    count = K // 4
    inverse = work[pl.ds(pl.multiple_of(own * count, count), count), K:] * scale
    width = 4 * BS
    mine, second, pair = slices
    for other, value in (
        (0, mine[...]),
        (2, second[...]),
        (1, pair[:K]),
        (3, pair[K:]),
    ):
        start = pl.multiple_of((own ^ other) * width, width)
        ortho_ref[:, pl.ds(start, width)] = dot_n(inverse, value)


def exchange(value, axis):
    return lax.ppermute(value, axis, [(0, 1), (1, 0)])


def to_all(value, axis):
    return lax.all_to_all(value, axis, 0, 0, tiled=True)


def filtered_basis(start_panel, tile_values, tile_rows, tile_cols, tile_counts):
    q = lax.axis_index("q")
    count_q = lax.axis_size("q")
    xh = lax.axis_index("xh")
    core = lax.axis_index("core")
    c = lax.axis_index("xl") * 2 + core
    quarter = TILE_CAP // 4

    even = [(i, i ^ 1) for i in range(count_q)]
    odd = [(i, (i + 1 if i % 2 else i - 1) % count_q) for i in range(count_q)]

    def halo(value):
        one = lax.ppermute(value, "q", even)
        two = lax.ppermute(value, "q", odd)
        return one, two

    count = 2 * count_q
    near = [(b, (b + 1 if b % 2 else b - 1) % count) for b in range(count)]
    diagonal = lax.ppermute(start_panel, ("q", "xh"), near)
    across = exchange(start_panel, "xh")
    one, two = halo(start_panel)
    ids = jnp.stack([q, xh, c])
    order = jax.ShapeDtypeStruct((3 * TILE_CAP + 4,), jnp.int32)
    split = jax.ShapeDtypeStruct((TILE_CAP, 2, BS, BS), jnp.bfloat16)
    own_tiles, piece, own_list = pl.pallas_call(
        functools.partial(own_kernel, count_q),
        out_shape=(split, jax.ShapeDtypeStruct((quarter, BS, BS), jnp.float32), order),
        in_specs=[SMEM] * 4 + [pl.BlockSpec(memory_space=pltpu.MemorySpace.HBM)],
        out_specs=(VMEM, VMEM, SMEM),
        scratch_shapes=[
            pltpu.VMEM((TILE_CAP, BS, BS), jnp.float32),
            pltpu.SemaphoreType.DMA((CHUNKS,)),
        ],
        compiler_params=pltpu.CompilerParams(vmem_limit_bytes=24 << 20),
        cost_estimate=pl.CostEstimate(flops=0, bytes_accessed=6 << 20, transcendentals=0),
        interpret=INTERPRET,
        name="own",
    )(ids, in_hbm(tile_rows), in_hbm(tile_cols), tile_counts, in_hbm(tile_values))
    first = lax.ppermute(piece, ("xh", "xl"), [(i, 3 - i) for i in range(4)])
    second = exchange(first, "xl")
    pair = jnp.concatenate([first, second], axis=0)
    far = exchange(pair, "core")
    notes = jnp.concatenate(
        [
            tile_rows.astype(jnp.float32)[None],
            tile_cols.astype(jnp.float32)[None],
            jnp.broadcast_to(tile_counts.astype(jnp.float32)[None], (1, TILE_CAP)),
        ],
        axis=0,
    )
    notes = jnp.pad(notes, ((0, COLS - 3), (0, BS - TILE_CAP)))
    half = jax.ShapeDtypeStruct((RB_DEV, COLS, BS), jnp.float32)
    mine, given, previous = call(
        functools.partial(first_kernel, count),
        (
            half,
            jax.ShapeDtypeStruct((RB_DEV + 1, COLS, BS), jnp.float32),
            jax.ShapeDtypeStruct((HALF, COLS, BS), jnp.float32),
        ),
        [
            ids, tile_rows, tile_cols, tile_counts,
            notes, start_panel, one, two, across, diagonal, own_tiles,
        ],
        [SMEM] * 4 + [VMEM] * 7,
        scratch=[
            pltpu.VMEM((5 * RB_DEV, 4 * COLS, BS), jnp.bfloat16),
            pltpu.VMEM((RB_DEV, 2 * COLS, BS), jnp.float32),
        ],
        flops=2 * TILE_CAP * 6 * COLS * BS * BS,
        moved=4 << 20,
    )
    got = exchange(given, "xh")
    current = jnp.concatenate([mine, got[:RB_DEV]], axis=0)
    other_tiles, other_list = pl.pallas_call(
        functools.partial(other_kernel, count_q),
        out_shape=(split, order),
        in_specs=[SMEM] * 2 + [VMEM] * 2,
        out_specs=(VMEM, SMEM),
        compiler_params=pltpu.CompilerParams(vmem_limit_bytes=24 << 20),
        cost_estimate=pl.CostEstimate(flops=0, bytes_accessed=6 << 20, transcendentals=0),
        interpret=INTERPRET,
        name="other",
    )(ids, got[RB_DEV, :3, :TILE_CAP], pair, far)
    lists = (own_list, other_list)
    for step in range(1, DEGREE):
        one, two = halo(current)
        final = step == DEGREE - 1
        tiles = (own_tiles, other_tiles, final)
        part = graph_part(lists, 0, current, (), *tiles)
        part = graph_part(lists, 1, one, (part,), *tiles)
        upcoming = graph_part(lists, 2, two, (part, previous), *tiles)
        previous, current = current, upcoming

    parts = to_all(current.reshape(8, 4, COLS, BS), GROUP)
    everything, gram = call(
        gram_kernel,
        (
            jax.ShapeDtypeStruct((K, 4 * BS), jnp.float32),
            jax.ShapeDtypeStruct((K, K), jnp.float32),
        ),
        [parts],
        [VMEM],
        flops=2 * K * K * 4 * BS * 6,
        moved=1 << 20,
    )
    second = exchange(everything, "xl")
    far_slices = exchange(jnp.concatenate([everything, second], axis=0), "core")
    rows = K // count_q if K >= count_q else 1
    spread = to_all(gram, "q").reshape(count_q, rows, K).sum(axis=0)
    spread = to_all(jnp.broadcast_to(spread[None], (8, rows, K)), GROUP).sum(axis=0)
    gram = to_all(jnp.broadcast_to(spread[None], (count_q, rows, K)), "q").reshape(K, K)

    total_rows = start_panel.shape[1] * count_q * 2
    factor, ortho_panel = call(
        functools.partial(factor_kernel, math.sqrt(total_rows)),
        (
            jax.ShapeDtypeStruct((K, K), jnp.float32),
            jax.ShapeDtypeStruct((K // 4, 16 * BS), jnp.float32),
        ),
        [c[None], gram, everything, second, far_slices],
        [SMEM] + [VMEM] * 4,
        scratch=[pltpu.VMEM((K, 2 * K), jnp.float32)],
        flops=2 * K * K * 4 * BS * 6,
        moved=1 << 20,
    )
    return (ortho_panel, factor)


def solution(mesh):
    grid = Mesh(
        mesh.devices.reshape(mesh.devices.shape[0] // 2, 2, 2, 2), ("q", "xh", "xl", "core")
    )
    blk = ("q", "xh")
    in_specs = (P(COL, blk), P(blk, None, None), P(blk), P(blk), P(blk))
    out_specs = (P(COL, blk), P())
    return jax.shard_map(
        filtered_basis, mesh=grid, in_specs=in_specs, out_specs=out_specs, check_vma=False
    )
```

```python
import functools
import math

import jax
import jax.numpy as jnp
from jax import lax
from jax.experimental import pallas as pl
from jax.experimental.pallas import tpu as pltpu
from jax.sharding import Mesh
from jax.sharding import PartitionSpec as P

BS = 128
K = 128
RB_DEV = 16
TILE_CAP = 24
REACH = 2
DEGREE = 4
COLS = 16
HALF = 2 * RB_DEV
UNROLL = 4
CHUNKS = 4
BLOCK = 32
FEW = 4
GROUP = ("xh", "xl", "core")
COL = ("xl", "core")
VMEM = pl.BlockSpec(memory_space=pltpu.VMEM)
SMEM = pl.BlockSpec(memory_space=pltpu.SMEM)
INTERPRET = False


def in_hbm(value):
    return value if INTERPRET else pltpu.with_memory_space_constraint(value, pltpu.MemorySpace.HBM)


def split_bf16(value):
    high = value.astype(jnp.bfloat16)
    low = (value - high.astype(jnp.float32)).astype(jnp.bfloat16)
    return high, low


def call(kernel, out_shape, operands, specs, scratch=(), flops=0, moved=0):
    outs = jax.tree.map(lambda s: VMEM, out_shape)
    return pl.pallas_call(
        kernel,
        out_shape=out_shape,
        in_specs=specs,
        out_specs=outs,
        scratch_shapes=list(scratch),
        compiler_params=pltpu.CompilerParams(vmem_limit_bytes=24 << 20),
        cost_estimate=pl.CostEstimate(flops=flops, bytes_accessed=moved, transcendentals=0),
        interpret=INTERPRET,
    )(*operands)


def sort_slots(ids, count_q, live, slot_of, lists):
    q, xh = ids[0], ids[1]

    def body(slot, fills):
        row, column, place = slot_of(slot)
        owner = column >> 4
        step = lax.rem((owner >> 1) - q + 1 + count_q, count_q)
        near = (step == 2) == ((q & 1) == 0)
        piece = jnp.where(step == 1, 0, jnp.where(near, 2, 1))
        local = ((owner & 1) ^ xh) * RB_DEV + (column & (RB_DEV - 1))
        fill = jnp.where(piece == 0, fills[0], jnp.where(piece == 1, fills[1], fills[2]))
        lists[piece * TILE_CAP + fill] = row + HALF * local + HALF * HALF * place
        return tuple(fills[k] + (piece == k).astype(jnp.int32) for k in range(3))

    zero = jnp.int32(0)
    fills = lax.fori_loop(0, live, body, (zero, zero, zero))
    for k in range(3):
        lists[3 * TILE_CAP + k] = fills[k]
    lists[3 * TILE_CAP + 3] = xh * RB_DEV


def split_into(value, out_ref, slot):
    high, low = split_bf16(value.T)
    out_ref[slot, 0] = high
    out_ref[slot, 1] = low


def own_kernel(count_q, ids, rows, cols, count, tiles, split_ref, lists, held, sems):
    chunk = TILE_CAP // CHUNKS
    copies = []
    for k in range(CHUNKS):
        part = pl.ds(k * chunk, chunk)
        copies.append(pltpu.make_async_copy(tiles.at[part], held.at[part], sems.at[k]))
        copies[-1].start()

    def slot_of(slot):
        return rows[slot] & (RB_DEV - 1), cols[slot], slot

    sort_slots(ids, count_q, count[0], slot_of, lists)
    for k in range(CHUNKS):
        copies[k].wait()

        def body(slot, carry):
            split_into(held[slot], split_ref, slot)
            return carry

        lax.fori_loop(k * chunk, (k + 1) * chunk, body, 0, unroll=2)


def other_kernel(count_q, ids, notes, pair, far, split_ref, lists):
    quarter = TILE_CAP // 4

    def slot_of(slot):
        row = (notes[0, slot].astype(jnp.int32) & (RB_DEV - 1)) + RB_DEV
        part = lax.div(slot, quarter)
        order = part ^ ids[2]
        order = (order & 1) * 2 + 1 - (order >> 1)
        return row, notes[1, slot].astype(jnp.int32), order * quarter + slot - part * quarter

    sort_slots(ids, count_q, notes[2, 0].astype(jnp.int32), slot_of, lists)
    for base, piece in ((0, pair), (2 * quarter, far)):
        def body(slot, carry, base=base, piece=piece):
            split_into(piece[slot], split_ref, base + slot)
            return carry

        lax.fori_loop(0, 2 * quarter, body, 0, unroll=2)


def dot_t(left, right, precision=None):
    return lax.dot_general(
        left,
        right,
        (((1,), (1,)), ((), ())),
        preferred_element_type=jnp.float32,
        precision=precision,
    )


def part_kernel(piece, final, *refs):
    own_list, other_list, source_ref, *middle, own_ref, other_ref, out_ref, window, total = refs

    def fill(block, carry):
        high, low = split_bf16(source_ref[block])
        window[block, 0:COLS] = high
        window[block, COLS : 2 * COLS] = low
        return carry

    lax.fori_loop(0, HALF, fill, 0, unroll=8)
    if piece == 0:
        total[...] = jnp.zeros_like(total)
    else:
        total[...] = middle[0][...]
    base = piece * TILE_CAP
    for lists, tiles in ((own_list, own_ref), (other_list, other_ref)):
        live = lists[3 * TILE_CAP + piece]

        def body(group, carry, lists=lists, tiles=tiles, live=live):
            terms, rows = [], []
            for inner in range(UNROLL):
                slot = group * UNROLL + inner
                entry = jnp.where(slot < live, lists[base + slot], 0)
                both = window[(entry // HALF) % HALF]
                place = entry // (HALF * HALF)
                wide = dot_b(both, tiles[place, 0])
                narrow = dot_b(both[:COLS], tiles[place, 1])
                term = wide[:COLS] + (wide[COLS:] + narrow)
                terms.append(jnp.where(slot < live, term, jnp.zeros_like(term)))
                rows.append(entry % HALF)
            for inner in range(UNROLL):
                total[rows[inner]] = total[rows[inner]] + terms[inner]
            return carry

        lax.fori_loop(0, (live + UNROLL - 1) // UNROLL, body, 0)
    if piece < 2:
        out_ref[...] = total[...]
        return
    prev_ref = middle[1]
    swap = own_list[3 * TILE_CAP + 3] if final else 0

    def finish(block, carry):
        source = block ^ swap if final else block
        out_ref[block] = 2.0 * total[source] - prev_ref[source]
        return carry

    lax.fori_loop(0, HALF, finish, 0, unroll=8)


def dot_b(left, right):
    return lax.dot_general(
        left, right, (((1,), (0,)), ((), ())), preferred_element_type=jnp.float32
    )


def first_kernel(count_b, *refs):
    ids, rows, cols, count, notes_ref, *refs = refs
    *pieces, tiles, mine_ref, given_ref, start_ref, window, total = refs
    q, xh = ids[0], ids[1]

    def place_of(column):
        offset = lax.rem((column >> 4) - 2 * q - xh + REACH + count_b, count_b)
        side = jnp.where((q & 1) == 0, 2 * REACH - offset, offset)
        place = jnp.where((offset & 1) == 1, jnp.where((offset == 3) == (xh == 0), 3, 4), 0)
        place = jnp.where(side == 0, 1, jnp.where(side == 4, 2, place))
        return place * RB_DEV + (column & (RB_DEV - 1))

    wide_cols = 2 * COLS
    for piece, ref in enumerate(pieces):
        for block in range(RB_DEV):
            high, low = split_bf16(ref[:, block * BS : (block + 1) * BS])
            window[piece * RB_DEV + block, 0:wide_cols] = high
            window[piece * RB_DEV + block, wide_cols : 2 * wide_cols] = low
    total[...] = jnp.zeros_like(total)
    live = count[0]
    upper = xh == 1

    def body(group, carry):
        terms = []
        for inner in range(UNROLL):
            slot = group * UNROLL + inner
            both = window[place_of(cols[slot])]
            wide = dot_b(both, tiles[slot, 0])
            narrow = dot_b(both[:wide_cols], tiles[slot, 1])
            term = wide[:wide_cols] + (wide[wide_cols:] + narrow)
            terms.append(jnp.where(slot < live, term, jnp.zeros_like(term)))
        for inner in range(UNROLL):
            row = rows[group * UNROLL + inner] & (RB_DEV - 1)
            total[row] = total[row] + terms[inner]
        return carry

    lax.fori_loop(0, (live + UNROLL - 1) // UNROLL, body, 0)
    for block in range(RB_DEV):
        value = total[block]
        mine_ref[block] = jnp.where(upper, value[COLS:], value[:COLS])
        given_ref[block] = jnp.where(upper, value[:COLS], value[COLS:])
        for half, ref in enumerate((pieces[0], pieces[3])):
            value = ref[:, block * BS : (block + 1) * BS]
            start_ref[half * RB_DEV + block] = jnp.where(upper, value[COLS:], value[:COLS])
    given_ref[RB_DEV] = notes_ref[...]


def graph_part(lists, piece, source, middle, own_tiles, other_tiles, final):
    operands = [*lists, source, *middle, own_tiles, other_tiles]
    return call(
        functools.partial(part_kernel, piece, final),
        jax.ShapeDtypeStruct((HALF, COLS, BS), jnp.float32),
        operands,
        [SMEM] * 2 + [VMEM] * (len(operands) - 2),
        scratch=[
            pltpu.VMEM((HALF, 2 * COLS, BS), jnp.bfloat16),
            pltpu.VMEM((HALF, COLS, BS), jnp.float32),
        ],
        flops=2 * TILE_CAP * 2 * COLS * BS * BS,
        moved=4 << 20,
    )


def gram_kernel(parts_ref, all_ref, gram_ref):
    for half in range(2):
        for c in range(4):
            for block in range(4):
                row = (2 * c + half) * COLS
                all_ref[row : row + COLS, block * BS : (block + 1) * BS] = parts_ref[
                    half * 4 + c, block
                ]
    value = all_ref[...]
    gram_ref[...] = dot_t(value, value, precision=lax.Precision.HIGHEST)


def dot_n(left, right):
    return lax.dot_general(
        left,
        right,
        (((1,), (0,)), ((), ())),
        preferred_element_type=jnp.float32,
        precision=lax.Precision.HIGHEST,
    )


def eliminate(value, size):
    shape = value.shape
    row = lax.broadcasted_iota(jnp.int32, shape, 0)
    for start in range(0, size, FEW):
        raw = [jnp.broadcast_to(value[:, start + b : start + b + 1], shape) for b in range(FEW)]
        lines = [jnp.broadcast_to(value[start + b : start + b + 1], shape) for b in range(FEW)]
        small = [
            [jnp.broadcast_to(raw[b][start + a : start + a + 1], shape) for b in range(a + 1)]
            for a in range(FEW)
        ]
        columns, ups = [], []
        for b in range(FEW):
            root = lax.rsqrt(small[b][b])
            for a in range(b + 1, FEW):
                small[a][b] = small[a][b] * root
            for a in range(b + 1, FEW):
                for c in range(b + 1, a + 1):
                    small[a][c] = small[a][c] - small[a][b] * small[c][b]
            column, up = raw[b], lines[b]
            for c in range(b):
                column = column - columns[c] * small[b][c]
                up = up - ups[c] * small[b][c]
            columns.append(column * root)
            ups.append(up * root)
        change = columns[0] * ups[0]
        for b in range(1, FEW):
            change = change + columns[b] * ups[b]
        value = jnp.where(row >= start + FEW, value - change, value)
        for b in range(FEW):
            value = jnp.where(row == start + b, ups[b], value)
    return value


def factor_kernel(scale, place_ref, gram_ref, *refs):
    *slices, factor_ref, ortho_ref, work = refs
    row = lax.broadcasted_iota(jnp.int32, (K, K), 0)
    lane = lax.broadcasted_iota(jnp.int32, (K, K), 1)
    work[:, :K] = gram_ref[...]
    work[:, K:] = (row == lane).astype(jnp.float32)
    small_row = lax.broadcasted_iota(jnp.int32, (BLOCK, K), 0)
    small_lane = lax.broadcasted_iota(jnp.int32, (BLOCK, K), 1)
    unit = (small_row + BLOCK == small_lane).astype(jnp.float32)
    for start in range(0, K, BLOCK):
        rows = slice(start, start + BLOCK)
        diagonal = work[rows, :K]
        if start:
            diagonal = pltpu.roll(diagonal, K - start, 1)
        done = eliminate(jnp.where(small_lane < BLOCK, diagonal, unit), BLOCK)
        inverse = pltpu.roll(done, K - BLOCK, 1)[:, :BLOCK]
        ups = dot_n(inverse, work[rows, :])
        work[rows, :] = ups
        below = start + BLOCK
        if below < K:
            change = dot_n(ups[:, :K].T, ups)
            work[below:, :] = work[below:, :] - change[below:]
    factor_ref[...] = (jnp.where(lane >= row, work[:, :K], 0.0) / scale).T
    own = place_ref[0]
    count = K // 4
    inverse = work[pl.ds(pl.multiple_of(own * count, count), count), K:] * scale
    width = 4 * BS
    mine, second, pair = slices
    for other, value in (
        (0, mine[...]),
        (2, second[...]),
        (1, pair[:K]),
        (3, pair[K:]),
    ):
        start = pl.multiple_of((own ^ other) * width, width)
        ortho_ref[:, pl.ds(start, width)] = dot_n(inverse, value)


def exchange(value, axis):
    return lax.ppermute(value, axis, [(0, 1), (1, 0)])


def to_all(value, axis):
    return lax.all_to_all(value, axis, 0, 0, tiled=True)


def filtered_basis(start_panel, tile_values, tile_rows, tile_cols, tile_counts):
    q = lax.axis_index("q")
    count_q = lax.axis_size("q")
    xh = lax.axis_index("xh")
    core = lax.axis_index("core")
    c = lax.axis_index("xl") * 2 + core
    quarter = TILE_CAP // 4

    even = [(i, i ^ 1) for i in range(count_q)]
    odd = [(i, (i + 1 if i % 2 else i - 1) % count_q) for i in range(count_q)]

    def halo(value):
        one = lax.ppermute(value, "q", even)
        two = lax.ppermute(value, "q", odd)
        return one, two

    count = 2 * count_q
    near = [(b, (b + 1 if b % 2 else b - 1) % count) for b in range(count)]
    diagonal = lax.ppermute(start_panel, ("q", "xh"), near)
    across = exchange(start_panel, "xh")
    one, two = halo(start_panel)
    ids = jnp.stack([q, xh, c])
    order = jax.ShapeDtypeStruct((3 * TILE_CAP + 4,), jnp.int32)
    split = jax.ShapeDtypeStruct((TILE_CAP, 2, BS, BS), jnp.bfloat16)
    own_tiles, own_list = pl.pallas_call(
        functools.partial(own_kernel, count_q),
        out_shape=(split, order),
        in_specs=[SMEM] * 4 + [pl.BlockSpec(memory_space=pltpu.MemorySpace.HBM)],
        out_specs=(VMEM, SMEM),
        scratch_shapes=[
            pltpu.VMEM((TILE_CAP, BS, BS), jnp.float32),
            pltpu.SemaphoreType.DMA((CHUNKS,)),
        ],
        compiler_params=pltpu.CompilerParams(vmem_limit_bytes=24 << 20),
        cost_estimate=pl.CostEstimate(flops=0, bytes_accessed=6 << 20, transcendentals=0),
        interpret=INTERPRET,
        name="own",
    )(ids, in_hbm(tile_rows), in_hbm(tile_cols), tile_counts, in_hbm(tile_values))
    piece = lax.dynamic_slice_in_dim(tile_values, c * quarter, quarter, 0)
    first = lax.ppermute(piece, ("xh", "xl"), [(i, 3 - i) for i in range(4)])
    second = exchange(first, "xl")
    pair = jnp.concatenate([first, second], axis=0)
    far = exchange(pair, "core")
    notes = jnp.concatenate(
        [
            tile_rows.astype(jnp.float32)[None],
            tile_cols.astype(jnp.float32)[None],
            jnp.broadcast_to(tile_counts.astype(jnp.float32)[None], (1, TILE_CAP)),
        ],
        axis=0,
    )
    notes = jnp.pad(notes, ((0, COLS - 3), (0, BS - TILE_CAP)))
    half = jax.ShapeDtypeStruct((RB_DEV, COLS, BS), jnp.float32)
    mine, given, previous = call(
        functools.partial(first_kernel, count),
        (
            half,
            jax.ShapeDtypeStruct((RB_DEV + 1, COLS, BS), jnp.float32),
            jax.ShapeDtypeStruct((HALF, COLS, BS), jnp.float32),
        ),
        [
            ids, tile_rows, tile_cols, tile_counts,
            notes, start_panel, one, two, across, diagonal, own_tiles,
        ],
        [SMEM] * 4 + [VMEM] * 7,
        scratch=[
            pltpu.VMEM((5 * RB_DEV, 4 * COLS, BS), jnp.bfloat16),
            pltpu.VMEM((RB_DEV, 2 * COLS, BS), jnp.float32),
        ],
        flops=2 * TILE_CAP * 6 * COLS * BS * BS,
        moved=4 << 20,
    )
    got = exchange(given, "xh")
    current = jnp.concatenate([mine, got[:RB_DEV]], axis=0)
    other_tiles, other_list = pl.pallas_call(
        functools.partial(other_kernel, count_q),
        out_shape=(split, order),
        in_specs=[SMEM] * 2 + [VMEM] * 2,
        out_specs=(VMEM, SMEM),
        compiler_params=pltpu.CompilerParams(vmem_limit_bytes=24 << 20),
        cost_estimate=pl.CostEstimate(flops=0, bytes_accessed=6 << 20, transcendentals=0),
        interpret=INTERPRET,
        name="other",
    )(ids, got[RB_DEV, :3, :TILE_CAP], pair, far)
    lists = (own_list, other_list)
    for step in range(1, DEGREE):
        two, one = halo(current)
        final = step == DEGREE - 1
        tiles = (own_tiles, other_tiles, final)
        part = graph_part(lists, 0, current, (), *tiles)
        part = graph_part(lists, 1, one, (part,), *tiles)
        upcoming = graph_part(lists, 2, two, (part, previous), *tiles)
        previous, current = current, upcoming

    parts = to_all(current.reshape(8, 4, COLS, BS), GROUP)
    everything, gram = call(
        gram_kernel,
        (
            jax.ShapeDtypeStruct((K, 4 * BS), jnp.float32),
            jax.ShapeDtypeStruct((K, K), jnp.float32),
        ),
        [parts],
        [VMEM],
        flops=2 * K * K * 4 * BS * 6,
        moved=1 << 20,
    )
    second = exchange(everything, "xl")
    far_slices = exchange(jnp.concatenate([everything, second], axis=0), "core")
    rows = K // count_q if K >= count_q else 1
    spread = to_all(gram, "q").reshape(count_q, rows, K).sum(axis=0)
    spread = to_all(jnp.broadcast_to(spread[None], (8, rows, K)), GROUP).sum(axis=0)
    gram = to_all(jnp.broadcast_to(spread[None], (count_q, rows, K)), "q").reshape(K, K)

    total_rows = start_panel.shape[1] * count_q * 2
    factor, ortho_panel = call(
        functools.partial(factor_kernel, math.sqrt(total_rows)),
        (
            jax.ShapeDtypeStruct((K, K), jnp.float32),
            jax.ShapeDtypeStruct((K // 4, 16 * BS), jnp.float32),
        ),
        [c[None], gram, everything, second, far_slices],
        [SMEM] + [VMEM] * 4,
        scratch=[pltpu.VMEM((K, 2 * K), jnp.float32)],
        flops=2 * K * K * 4 * BS * 6,
        moved=1 << 20,
    )
    return (ortho_panel, factor)


def solution(mesh):
    grid = Mesh(
        mesh.devices.reshape(mesh.devices.shape[0] // 2, 2, 2, 2), ("q", "xh", "xl", "core")
    )
    blk = ("q", "xh")
    in_specs = (P(COL, blk), P(blk, None, None), P(blk), P(blk), P(blk))
    out_specs = (P(COL, blk), P())
    return jax.shard_map(
        filtered_basis, mesh=grid, in_specs=in_specs, out_specs=out_specs, check_vma=False
    )
```

```python
import functools
import math

import jax
import jax.numpy as jnp
from jax import lax
from jax.experimental import pallas as pl
from jax.experimental.pallas import tpu as pltpu
from jax.sharding import Mesh
from jax.sharding import PartitionSpec as P

BS = 128
K = 128
RB_DEV = 16
TILE_CAP = 24
REACH = 2
DEGREE = 4
COLS = 16
HALF = 2 * RB_DEV
UNROLL = 4
CHUNKS = 4
BLOCK = 32
FEW = 4
GROUP = ("xh", "xl", "core")
COL = ("xl", "core")
VMEM = pl.BlockSpec(memory_space=pltpu.VMEM)
SMEM = pl.BlockSpec(memory_space=pltpu.SMEM)
INTERPRET = False


def in_hbm(value):
    return value if INTERPRET else pltpu.with_memory_space_constraint(value, pltpu.MemorySpace.HBM)


def split_bf16(value):
    high = value.astype(jnp.bfloat16)
    low = (value - high.astype(jnp.float32)).astype(jnp.bfloat16)
    return high, low


def call(kernel, out_shape, operands, specs, scratch=(), flops=0, moved=0):
    outs = jax.tree.map(lambda s: VMEM, out_shape)
    return pl.pallas_call(
        kernel,
        out_shape=out_shape,
        in_specs=specs,
        out_specs=outs,
        scratch_shapes=list(scratch),
        compiler_params=pltpu.CompilerParams(vmem_limit_bytes=24 << 20),
        cost_estimate=pl.CostEstimate(flops=flops, bytes_accessed=moved, transcendentals=0),
        interpret=INTERPRET,
    )(*operands)


def sort_slots(ids, count_q, live, slot_of, lists):
    q, xh = ids[0], ids[1]

    def body(slot, fills):
        row, column, place = slot_of(slot)
        owner = column >> 4
        step = lax.rem((owner >> 1) - q + 1 + count_q, count_q)
        far = (step != 1).astype(jnp.int32)
        even = jnp.where((step == 2) == ((q & 1) == 0), far, 0)
        local = even * HALF + ((owner & 1) ^ xh) * RB_DEV + (column & (RB_DEV - 1))
        fill = jnp.where(far == 1, fills[1], fills[0])
        lists[far * TILE_CAP + fill] = row + HALF * local + 2 * HALF * HALF * place
        return fills[0] + 1 - far, fills[1] + far

    zero = jnp.int32(0)
    fills = lax.fori_loop(0, live, body, (zero, zero))
    for k in range(2):
        lists[2 * TILE_CAP + k] = fills[k]
    lists[2 * TILE_CAP + 2] = xh * RB_DEV


def split_into(value, out_ref, slot):
    high, low = split_bf16(value.T)
    out_ref[slot, 0] = high
    out_ref[slot, 1] = low


def own_kernel(count_q, ids, rows, cols, count, tiles, split_ref, lists, held, sems):
    chunk = TILE_CAP // CHUNKS
    copies = []
    for k in range(CHUNKS):
        part = pl.ds(k * chunk, chunk)
        copies.append(pltpu.make_async_copy(tiles.at[part], held.at[part], sems.at[k]))
        copies[-1].start()

    def slot_of(slot):
        return rows[slot] & (RB_DEV - 1), cols[slot], slot

    sort_slots(ids, count_q, count[0], slot_of, lists)
    for k in range(CHUNKS):
        copies[k].wait()

        def body(slot, carry):
            split_into(held[slot], split_ref, slot)
            return carry

        lax.fori_loop(k * chunk, (k + 1) * chunk, body, 0, unroll=2)


def partner_kernel(count_q, ids, notes, lists):
    quarter = TILE_CAP // 4

    def slot_of(slot):
        row = (notes[0, slot].astype(jnp.int32) & (RB_DEV - 1)) + RB_DEV
        part = lax.div(slot, quarter)
        order = part ^ ids[2]
        order = (order & 1) * 2 + 1 - (order >> 1)
        return row, notes[1, slot].astype(jnp.int32), order * quarter + slot - part * quarter

    sort_slots(ids, count_q, notes[2, 0].astype(jnp.int32), slot_of, lists)


def other_kernel(pair, far, split_ref):
    quarter = TILE_CAP // 4
    for k, (piece, start) in enumerate(((pair, 0), (pair, quarter + 1), (far, 0), (far, quarter + 1))):
        def body(slot, carry, k=k, piece=piece, start=start):
            split_into(piece[start + slot], split_ref, k * quarter + slot)
            return carry

        lax.fori_loop(0, quarter, body, 0, unroll=2)


def dot_t(left, right, precision=None):
    return lax.dot_general(
        left,
        right,
        (((1,), (1,)), ((), ())),
        preferred_element_type=jnp.float32,
        precision=precision,
    )


def part_kernel(halos, final, *refs):
    own_list, other_list, *refs = refs
    sources, refs = (refs[:2], refs[2:]) if halos else (refs[:1], refs[1:])
    *middle, own_ref, other_ref, out_ref, window, total = refs
    for base, source_ref in enumerate(sources):
        def fill(block, carry, base=base, source_ref=source_ref):
            high, low = split_bf16(source_ref[block])
            window[base * HALF + block, 0:COLS] = high
            window[base * HALF + block, COLS : 2 * COLS] = low
            return carry

        lax.fori_loop(0, HALF, fill, 0, unroll=8)
    if halos:
        total[...] = middle[0][...]
    else:
        total[...] = jnp.zeros_like(total)
    base = TILE_CAP if halos else 0
    for lists, tiles in ((own_list, own_ref), (other_list, other_ref)):
        live = lists[2 * TILE_CAP + int(halos)]

        def body(group, carry, lists=lists, tiles=tiles, live=live):
            terms, rows = [], []
            for inner in range(UNROLL):
                slot = group * UNROLL + inner
                entry = jnp.where(slot < live, lists[base + slot], 0)
                both = window[(entry >> 5) & (2 * HALF - 1)]
                place = entry >> 11
                wide = dot_b(both, tiles[place, 0])
                narrow = dot_b(both[:COLS], tiles[place, 1])
                term = wide[:COLS] + (wide[COLS:] + narrow)
                terms.append(jnp.where(slot < live, term, jnp.zeros_like(term)))
                rows.append(entry & (HALF - 1))
            for inner in range(UNROLL):
                total[rows[inner]] = total[rows[inner]] + terms[inner]
            return carry

        lax.fori_loop(0, (live + UNROLL - 1) // UNROLL, body, 0)
    if not halos:
        out_ref[...] = total[...]
        return
    prev_ref = middle[1]
    swap = own_list[2 * TILE_CAP + 2] if final else 0

    def finish(block, carry):
        source = block ^ swap if final else block
        out_ref[block] = 2.0 * total[source] - prev_ref[source]
        return carry

    lax.fori_loop(0, HALF, finish, 0, unroll=8)


def dot_b(left, right):
    return lax.dot_general(
        left, right, (((1,), (0,)), ((), ())), preferred_element_type=jnp.float32
    )


def first_kernel(count_b, *refs):
    ids, rows, cols, count, *refs = refs
    *pieces, tiles, mine_ref, given_ref, start_ref, window, total = refs
    q, xh = ids[0], ids[1]

    def place_of(column):
        offset = lax.rem((column >> 4) - 2 * q - xh + REACH + count_b, count_b)
        side = jnp.where((q & 1) == 0, 2 * REACH - offset, offset)
        place = jnp.where((offset & 1) == 1, jnp.where((offset == 3) == (xh == 0), 3, 4), 0)
        place = jnp.where(side == 0, 1, jnp.where(side == 4, 2, place))
        return place * RB_DEV + (column & (RB_DEV - 1))

    wide_cols = 2 * COLS
    for piece, ref in enumerate(pieces):
        for block in range(RB_DEV):
            high, low = split_bf16(ref[:, block * BS : (block + 1) * BS])
            window[piece * RB_DEV + block, 0:wide_cols] = high
            window[piece * RB_DEV + block, wide_cols : 2 * wide_cols] = low
    total[...] = jnp.zeros_like(total)
    live = count[0]
    upper = xh == 1

    def body(group, carry):
        terms = []
        for inner in range(UNROLL):
            slot = group * UNROLL + inner
            both = window[place_of(cols[slot])]
            wide = dot_b(both, tiles[slot, 0])
            narrow = dot_b(both[:wide_cols], tiles[slot, 1])
            term = wide[:wide_cols] + (wide[wide_cols:] + narrow)
            terms.append(jnp.where(slot < live, term, jnp.zeros_like(term)))
        for inner in range(UNROLL):
            row = rows[group * UNROLL + inner] & (RB_DEV - 1)
            total[row] = total[row] + terms[inner]
        return carry

    lax.fori_loop(0, (live + UNROLL - 1) // UNROLL, body, 0)
    for block in range(RB_DEV):
        value = total[block]
        mine_ref[block] = jnp.where(upper, value[COLS:], value[:COLS])
        given_ref[block] = jnp.where(upper, value[:COLS], value[COLS:])
        for half, ref in enumerate((pieces[0], pieces[3])):
            value = ref[:, block * BS : (block + 1) * BS]
            start_ref[half * RB_DEV + block] = jnp.where(upper, value[COLS:], value[:COLS])


def graph_part(lists, sources, middle, own_tiles, other_tiles, final):
    halos = len(sources) == 2
    operands = [*lists, *sources, *middle, own_tiles, other_tiles]
    return call(
        functools.partial(part_kernel, halos, final),
        jax.ShapeDtypeStruct((HALF, COLS, BS), jnp.float32),
        operands,
        [SMEM] * 2 + [VMEM] * (len(operands) - 2),
        scratch=[
            pltpu.VMEM((len(sources) * HALF, 2 * COLS, BS), jnp.bfloat16),
            pltpu.VMEM((HALF, COLS, BS), jnp.float32),
        ],
        flops=2 * TILE_CAP * 2 * COLS * BS * BS,
        moved=4 << 20,
    )


def gram_kernel(parts_ref, all_ref, gram_ref):
    for half in range(2):
        for c in range(4):
            for block in range(4):
                row = (2 * c + half) * COLS
                all_ref[row : row + COLS, block * BS : (block + 1) * BS] = parts_ref[
                    half * 4 + c, block
                ]
    value = all_ref[...]
    gram_ref[...] = dot_t(value, value, precision=lax.Precision.HIGHEST)


def dot_n(left, right):
    return lax.dot_general(
        left,
        right,
        (((1,), (0,)), ((), ())),
        preferred_element_type=jnp.float32,
        precision=lax.Precision.HIGHEST,
    )


def eliminate(value, size):
    shape = value.shape
    row = lax.broadcasted_iota(jnp.int32, shape, 0)
    for start in range(0, size, FEW):
        raw = [jnp.broadcast_to(value[:, start + b : start + b + 1], shape) for b in range(FEW)]
        lines = [jnp.broadcast_to(value[start + b : start + b + 1], shape) for b in range(FEW)]
        small = [
            [jnp.broadcast_to(raw[b][start + a : start + a + 1], shape) for b in range(a + 1)]
            for a in range(FEW)
        ]
        columns, ups = [], []
        for b in range(FEW):
            root = lax.rsqrt(small[b][b])
            for a in range(b + 1, FEW):
                small[a][b] = small[a][b] * root
            for a in range(b + 1, FEW):
                for c in range(b + 1, a + 1):
                    small[a][c] = small[a][c] - small[a][b] * small[c][b]
            column, up = raw[b], lines[b]
            for c in range(b):
                column = column - columns[c] * small[b][c]
                up = up - ups[c] * small[b][c]
            columns.append(column * root)
            ups.append(up * root)
        change = columns[0] * ups[0]
        for b in range(1, FEW):
            change = change + columns[b] * ups[b]
        value = jnp.where(row >= start + FEW, value - change, value)
        for b in range(FEW):
            value = jnp.where(row == start + b, ups[b], value)
    return value


def factor_kernel(scale, place_ref, gram_ref, *refs):
    *slices, factor_ref, ortho_ref, work = refs
    row = lax.broadcasted_iota(jnp.int32, (K, K), 0)
    lane = lax.broadcasted_iota(jnp.int32, (K, K), 1)
    work[:, :K] = gram_ref[...]
    work[:, K:] = (row == lane).astype(jnp.float32)
    small_row = lax.broadcasted_iota(jnp.int32, (BLOCK, K), 0)
    small_lane = lax.broadcasted_iota(jnp.int32, (BLOCK, K), 1)
    unit = (small_row + BLOCK == small_lane).astype(jnp.float32)
    for start in range(0, K, BLOCK):
        rows = slice(start, start + BLOCK)
        diagonal = work[rows, :K]
        if start:
            diagonal = pltpu.roll(diagonal, K - start, 1)
        done = eliminate(jnp.where(small_lane < BLOCK, diagonal, unit), BLOCK)
        inverse = pltpu.roll(done, K - BLOCK, 1)[:, :BLOCK]
        ups = dot_n(inverse, work[rows, :])
        work[rows, :] = ups
        below = start + BLOCK
        if below < K:
            change = dot_n(ups[:, :K].T, ups)
            work[below:, :] = work[below:, :] - change[below:]
    factor_ref[...] = (jnp.where(lane >= row, work[:, :K], 0.0) / scale).T
    own = place_ref[0]
    count = K // 4
    inverse = work[pl.ds(pl.multiple_of(own * count, count), count), K:] * scale
    inverse_high, inverse_low = split_bf16(inverse)
    both = jnp.concatenate([inverse_high, inverse_low], axis=0)
    width = 4 * BS
    mine, second, pair = slices
    for other, value in (
        (0, mine[...]),
        (2, second[...]),
        (1, pair[:K]),
        (3, pair[K:]),
    ):
        start = pl.multiple_of((own ^ other) * width, width)
        high, low = split_bf16(value)
        wide = dot_b(both, high)
        product = wide[:count] + (wide[count:] + dot_b(inverse_high, low))
        ortho_ref[:, pl.ds(start, width)] = product


def exchange(value, axis):
    return lax.ppermute(value, axis, [(0, 1), (1, 0)])


def to_all(value, axis):
    return lax.all_to_all(value, axis, 0, 0, tiled=True)


def filtered_basis(start_panel, tile_values, tile_rows, tile_cols, tile_counts):
    q = lax.axis_index("q")
    count_q = lax.axis_size("q")
    xh = lax.axis_index("xh")
    core = lax.axis_index("core")
    c = lax.axis_index("xl") * 2 + core
    quarter = TILE_CAP // 4

    even = [(i, i ^ 1) for i in range(count_q)]
    odd = [(i, (i + 1 if i % 2 else i - 1) % count_q) for i in range(count_q)]

    def halo(value):
        one = lax.ppermute(value, "q", even)
        two = lax.ppermute(value, "q", odd)
        return one, two

    count = 2 * count_q
    near = [(b, (b + 1 if b % 2 else b - 1) % count) for b in range(count)]
    diagonal = lax.ppermute(start_panel, ("q", "xh"), near)
    across = exchange(start_panel, "xh")
    one, two = halo(start_panel)
    ids = jnp.stack([q, xh, c])
    order = jax.ShapeDtypeStruct((2 * TILE_CAP + 3,), jnp.int32)
    split = jax.ShapeDtypeStruct((TILE_CAP, 2, BS, BS), jnp.bfloat16)
    own_tiles, own_list = pl.pallas_call(
        functools.partial(own_kernel, count_q),
        out_shape=(split, order),
        in_specs=[SMEM] * 4 + [pl.BlockSpec(memory_space=pltpu.MemorySpace.HBM)],
        out_specs=(VMEM, SMEM),
        scratch_shapes=[
            pltpu.VMEM((TILE_CAP, BS, BS), jnp.float32),
            pltpu.SemaphoreType.DMA((CHUNKS,)),
        ],
        compiler_params=pltpu.CompilerParams(vmem_limit_bytes=24 << 20),
        cost_estimate=pl.CostEstimate(flops=0, bytes_accessed=6 << 20, transcendentals=0),
        interpret=INTERPRET,
        name="own",
    )(ids, in_hbm(tile_rows), in_hbm(tile_cols), tile_counts, in_hbm(tile_values))
    piece = lax.dynamic_slice_in_dim(tile_values, c * quarter, quarter, 0)
    notes = jnp.concatenate(
        [
            tile_rows.astype(jnp.float32)[None],
            tile_cols.astype(jnp.float32)[None],
            jnp.broadcast_to(tile_counts.astype(jnp.float32)[None], (1, TILE_CAP)),
        ],
        axis=0,
    )
    notes = jnp.pad(notes, ((0, BS - 3), (0, BS - TILE_CAP)))
    piece = jnp.concatenate([piece, notes[None]], axis=0)
    first = lax.ppermute(piece, ("xh", "xl"), [(i, 3 - i) for i in range(4)])
    second = exchange(first, "xl")
    pair = jnp.concatenate([first, second], axis=0)
    far = exchange(pair, "core")
    half = jax.ShapeDtypeStruct((RB_DEV, COLS, BS), jnp.float32)
    mine, given, previous = call(
        functools.partial(first_kernel, count),
        (
            half,
            half,
            jax.ShapeDtypeStruct((HALF, COLS, BS), jnp.float32),
        ),
        [
            ids, tile_rows, tile_cols, tile_counts,
            start_panel, one, two, across, diagonal, own_tiles,
        ],
        [SMEM] * 4 + [VMEM] * 6,
        scratch=[
            pltpu.VMEM((5 * RB_DEV, 4 * COLS, BS), jnp.bfloat16),
            pltpu.VMEM((RB_DEV, 2 * COLS, BS), jnp.float32),
        ],
        flops=2 * TILE_CAP * 6 * COLS * BS * BS,
        moved=4 << 20,
    )
    got = exchange(given, "xh")
    current = jnp.concatenate([mine, got], axis=0)
    other_list = pl.pallas_call(
        functools.partial(partner_kernel, count_q),
        out_shape=order,
        in_specs=[SMEM] * 2,
        out_specs=SMEM,
        interpret=INTERPRET,
        name="partner",
    )(ids, first[quarter, :3, :TILE_CAP])
    other_tiles = call(other_kernel, split, [pair, far], [VMEM] * 2, moved=6 << 20)
    lists = (own_list, other_list)
    for step in range(1, DEGREE):
        even_half, odd_half = halo(current)
        tiles = (own_tiles, other_tiles, step == DEGREE - 1)
        part = graph_part(lists, (current,), (), *tiles)
        upcoming = graph_part(lists, (odd_half, even_half), (part, previous), *tiles)
        previous, current = current, upcoming

    parts = to_all(current.reshape(8, 4, COLS, BS), GROUP)
    everything, gram = call(
        gram_kernel,
        (
            jax.ShapeDtypeStruct((K, 4 * BS), jnp.float32),
            jax.ShapeDtypeStruct((K, K), jnp.float32),
        ),
        [parts],
        [VMEM],
        flops=2 * K * K * 4 * BS * 6,
        moved=1 << 20,
    )
    second = exchange(everything, "xl")
    far_slices = exchange(jnp.concatenate([everything, second], axis=0), "core")
    rows = K // count_q if K >= count_q else 1
    spread = to_all(gram, "q").reshape(count_q, rows, K).sum(axis=0)
    spread = to_all(jnp.broadcast_to(spread[None], (8, rows, K)), GROUP).sum(axis=0)
    gram = to_all(jnp.broadcast_to(spread[None], (count_q, rows, K)), "q").reshape(K, K)

    total_rows = start_panel.shape[1] * count_q * 2
    factor, ortho_panel = call(
        functools.partial(factor_kernel, math.sqrt(total_rows)),
        (
            jax.ShapeDtypeStruct((K, K), jnp.float32),
            jax.ShapeDtypeStruct((K // 4, 16 * BS), jnp.float32),
        ),
        [c[None], gram, everything, second, far_slices],
        [SMEM] + [VMEM] * 4,
        scratch=[pltpu.VMEM((K, 2 * K), jnp.float32)],
        flops=2 * K * K * 4 * BS * 6,
        moved=1 << 20,
    )
    return (ortho_panel, factor)


def solution(mesh):
    grid = Mesh(
        mesh.devices.reshape(mesh.devices.shape[0] // 2, 2, 2, 2), ("q", "xh", "xl", "core")
    )
    blk = ("q", "xh")
    in_specs = (P(COL, blk), P(blk, None, None), P(blk), P(blk), P(blk))
    out_specs = (P(COL, blk), P())
    return jax.shard_map(
        filtered_basis, mesh=grid, in_specs=in_specs, out_specs=out_specs, check_vma=False
    )
```

```python
import functools
import math

import jax
import jax.numpy as jnp
from jax import lax
from jax.experimental import pallas as pl
from jax.experimental.pallas import tpu as pltpu
from jax.sharding import Mesh
from jax.sharding import PartitionSpec as P

BS = 128
K = 128
RB_DEV = 16
TILE_CAP = 24
REACH = 2
DEGREE = 4
COLS = 16
HALF = 2 * RB_DEV
UNROLL = 4
CHUNKS = 4
BLOCK = 32
FEW = 4
GROUP = ("xh", "xl", "core")
COL = ("xl", "core")
VMEM = pl.BlockSpec(memory_space=pltpu.VMEM)
SMEM = pl.BlockSpec(memory_space=pltpu.SMEM)
INTERPRET = False


def in_hbm(value):
    return value if INTERPRET else pltpu.with_memory_space_constraint(value, pltpu.MemorySpace.HBM)


def split_bf16(value):
    high = value.astype(jnp.bfloat16)
    low = (value - high.astype(jnp.float32)).astype(jnp.bfloat16)
    return high, low


def call(kernel, out_shape, operands, specs, scratch=(), flops=0, moved=0):
    outs = jax.tree.map(lambda s: VMEM, out_shape)
    return pl.pallas_call(
        kernel,
        out_shape=out_shape,
        in_specs=specs,
        out_specs=outs,
        scratch_shapes=list(scratch),
        compiler_params=pltpu.CompilerParams(vmem_limit_bytes=24 << 20),
        cost_estimate=pl.CostEstimate(flops=flops, bytes_accessed=moved, transcendentals=0),
        interpret=INTERPRET,
    )(*operands)


def sort_slots(ids, count_q, live, slot_of, lists):
    q, xh = ids[0], ids[1]

    def body(slot, fills):
        row, column, place = slot_of(slot)
        owner = column >> 4
        step = lax.rem((owner >> 1) - q + 1 + count_q, count_q)
        far = (step != 1).astype(jnp.int32)
        even = jnp.where((step == 2) == ((q & 1) == 0), far, 0)
        local = even * HALF + ((owner & 1) ^ xh) * RB_DEV + (column & (RB_DEV - 1))
        fill = jnp.where(far == 1, fills[1], fills[0])
        lists[far * TILE_CAP + fill] = row + HALF * local + 2 * HALF * HALF * place
        return fills[0] + 1 - far, fills[1] + far

    zero = jnp.int32(0)
    fills = lax.fori_loop(0, live, body, (zero, zero))
    for k in range(2):
        lists[2 * TILE_CAP + k] = fills[k]
    lists[2 * TILE_CAP + 2] = xh * RB_DEV


def split_into(value, out_ref, slot):
    high, low = split_bf16(value.T)
    out_ref[slot, 0] = high
    out_ref[slot, 1] = low


def own_kernel(count_q, ids, rows, cols, count, tiles, split_ref, lists, held, sems):
    chunk = TILE_CAP // CHUNKS
    copies = []
    for k in range(CHUNKS):
        part = pl.ds(k * chunk, chunk)
        copies.append(pltpu.make_async_copy(tiles.at[part], held.at[part], sems.at[k]))
        copies[-1].start()

    def slot_of(slot):
        return rows[slot] & (RB_DEV - 1), cols[slot], slot

    sort_slots(ids, count_q, count[0], slot_of, lists)
    for k in range(CHUNKS):
        copies[k].wait()

        def body(slot, carry):
            split_into(held[slot], split_ref, slot)
            return carry

        lax.fori_loop(k * chunk, (k + 1) * chunk, body, 0, unroll=2)


def cut_kernel(ids, count, rows, cols, tiles, piece_ref, sem):
    quarter = TILE_CAP // 4
    source = tiles.at[pl.ds(ids[2] * quarter, quarter)]
    copy = pltpu.make_async_copy(source, piece_ref.at[pl.ds(0, quarter)], sem)
    copy.start()
    piece_ref[quarter] = jnp.zeros((BS, BS), jnp.float32)
    piece_ref[quarter, 0:1, 0:TILE_CAP] = rows[...].astype(jnp.float32)
    piece_ref[quarter, 1:2, 0:TILE_CAP] = cols[...].astype(jnp.float32)
    piece_ref[quarter, 2:3, 0:TILE_CAP] = jnp.full((1, TILE_CAP), count[0].astype(jnp.float32))
    copy.wait()


def partner_kernel(count_q, ids, first, lists, notes, sem):
    quarter = TILE_CAP // 4
    copy = pltpu.make_async_copy(first.at[quarter, pl.ds(0, 8)], notes, sem)
    copy.start()
    copy.wait()

    def slot_of(slot):
        row = (notes[0, slot].astype(jnp.int32) & (RB_DEV - 1)) + RB_DEV
        part = lax.div(slot, quarter)
        order = part ^ ids[2]
        order = (order & 1) * 2 + 1 - (order >> 1)
        return row, notes[1, slot].astype(jnp.int32), order * quarter + slot - part * quarter

    sort_slots(ids, count_q, notes[2, 0].astype(jnp.int32), slot_of, lists)


def other_kernel(pair, far, split_ref):
    quarter = TILE_CAP // 4
    for k, (piece, start) in enumerate(((pair, 0), (pair, quarter + 1), (far, 0), (far, quarter + 1))):
        def body(slot, carry, k=k, piece=piece, start=start):
            split_into(piece[start + slot], split_ref, k * quarter + slot)
            return carry

        lax.fori_loop(0, quarter, body, 0, unroll=2)


def dot_t(left, right, precision=None):
    return lax.dot_general(
        left,
        right,
        (((1,), (1,)), ((), ())),
        preferred_element_type=jnp.float32,
        precision=precision,
    )


def part_kernel(halos, final, *refs):
    own_list, other_list, *refs = refs
    sources, refs = (refs[:2], refs[2:]) if halos else (refs[:1], refs[1:])
    *middle, own_ref, other_ref, out_ref, window, total = refs
    for base, source_ref in enumerate(sources):
        def fill(block, carry, base=base, source_ref=source_ref):
            high, low = split_bf16(source_ref[block])
            window[base * HALF + block, 0:COLS] = high
            window[base * HALF + block, COLS : 2 * COLS] = low
            return carry

        lax.fori_loop(0, HALF, fill, 0, unroll=8)
    if halos:
        total[...] = middle[0][...]
    else:
        total[...] = jnp.zeros_like(total)
    base = TILE_CAP if halos else 0
    for lists, tiles in ((own_list, own_ref), (other_list, other_ref)):
        live = lists[2 * TILE_CAP + int(halos)]

        def body(group, carry, lists=lists, tiles=tiles, live=live):
            terms, rows = [], []
            for inner in range(UNROLL):
                slot = group * UNROLL + inner
                entry = jnp.where(slot < live, lists[base + slot], 0)
                both = window[(entry >> 5) & (2 * HALF - 1)]
                place = entry >> 11
                wide = dot_b(both, tiles[place, 0])
                narrow = dot_b(both[:COLS], tiles[place, 1])
                term = wide[:COLS] + (wide[COLS:] + narrow)
                terms.append(jnp.where(slot < live, term, jnp.zeros_like(term)))
                rows.append(entry & (HALF - 1))
            for inner in range(UNROLL):
                total[rows[inner]] = total[rows[inner]] + terms[inner]
            return carry

        lax.fori_loop(0, (live + UNROLL - 1) // UNROLL, body, 0)
    if not halos:
        out_ref[...] = total[...]
        return
    prev_ref = middle[1]
    swap = own_list[2 * TILE_CAP + 2] if final else 0

    def finish(block, carry):
        source = block ^ swap if final else block
        out_ref[block] = 2.0 * total[source] - prev_ref[source]
        return carry

    lax.fori_loop(0, HALF, finish, 0, unroll=8)


def dot_b(left, right):
    return lax.dot_general(
        left, right, (((1,), (0,)), ((), ())), preferred_element_type=jnp.float32
    )


def first_kernel(count_b, *refs):
    ids, rows, cols, count, *refs = refs
    *pieces, tiles, mine_ref, given_ref, start_ref, window, total = refs
    q, xh = ids[0], ids[1]

    def place_of(column):
        offset = lax.rem((column >> 4) - 2 * q - xh + REACH + count_b, count_b)
        side = jnp.where((q & 1) == 0, 2 * REACH - offset, offset)
        place = jnp.where((offset & 1) == 1, jnp.where((offset == 3) == (xh == 0), 3, 4), 0)
        place = jnp.where(side == 0, 1, jnp.where(side == 4, 2, place))
        return place * RB_DEV + (column & (RB_DEV - 1))

    wide_cols = 2 * COLS
    for piece, ref in enumerate(pieces):
        for block in range(RB_DEV):
            high, low = split_bf16(ref[:, block * BS : (block + 1) * BS])
            window[piece * RB_DEV + block, 0:wide_cols] = high
            window[piece * RB_DEV + block, wide_cols : 2 * wide_cols] = low
    total[...] = jnp.zeros_like(total)
    live = count[0]
    upper = xh == 1

    def body(group, carry):
        terms = []
        for inner in range(UNROLL):
            slot = group * UNROLL + inner
            both = window[place_of(cols[slot])]
            wide = dot_b(both, tiles[slot, 0])
            narrow = dot_b(both[:wide_cols], tiles[slot, 1])
            term = wide[:wide_cols] + (wide[wide_cols:] + narrow)
            terms.append(jnp.where(slot < live, term, jnp.zeros_like(term)))
        for inner in range(UNROLL):
            row = rows[group * UNROLL + inner] & (RB_DEV - 1)
            total[row] = total[row] + terms[inner]
        return carry

    lax.fori_loop(0, (live + UNROLL - 1) // UNROLL, body, 0)
    for block in range(RB_DEV):
        value = total[block]
        mine_ref[block] = jnp.where(upper, value[COLS:], value[:COLS])
        given_ref[block] = jnp.where(upper, value[:COLS], value[COLS:])
        for half, ref in enumerate((pieces[0], pieces[3])):
            value = ref[:, block * BS : (block + 1) * BS]
            start_ref[half * RB_DEV + block] = jnp.where(upper, value[COLS:], value[:COLS])


def graph_part(lists, sources, middle, own_tiles, other_tiles, final):
    halos = len(sources) == 2
    operands = [*lists, *sources, *middle, own_tiles, other_tiles]
    return call(
        functools.partial(part_kernel, halos, final),
        jax.ShapeDtypeStruct((HALF, COLS, BS), jnp.float32),
        operands,
        [SMEM] * 2 + [VMEM] * (len(operands) - 2),
        scratch=[
            pltpu.VMEM((len(sources) * HALF, 2 * COLS, BS), jnp.bfloat16),
            pltpu.VMEM((HALF, COLS, BS), jnp.float32),
        ],
        flops=2 * TILE_CAP * 2 * COLS * BS * BS,
        moved=4 << 20,
    )


def gram_kernel(parts_ref, all_ref, gram_ref):
    for half in range(2):
        for c in range(4):
            for block in range(4):
                row = (2 * c + half) * COLS
                all_ref[row : row + COLS, block * BS : (block + 1) * BS] = parts_ref[
                    half * 4 + c, block
                ]
    value = all_ref[...]
    gram_ref[...] = dot_t(value, value, precision=lax.Precision.HIGHEST)


def dot_n(left, right):
    return lax.dot_general(
        left,
        right,
        (((1,), (0,)), ((), ())),
        preferred_element_type=jnp.float32,
        precision=lax.Precision.HIGHEST,
    )


def eliminate(value, size):
    shape = value.shape
    row = lax.broadcasted_iota(jnp.int32, shape, 0)
    for start in range(0, size, FEW):
        raw = [jnp.broadcast_to(value[:, start + b : start + b + 1], shape) for b in range(FEW)]
        lines = [jnp.broadcast_to(value[start + b : start + b + 1], shape) for b in range(FEW)]
        small = [
            [jnp.broadcast_to(raw[b][start + a : start + a + 1], shape) for b in range(a + 1)]
            for a in range(FEW)
        ]
        columns, ups = [], []
        for b in range(FEW):
            root = lax.rsqrt(small[b][b])
            for a in range(b + 1, FEW):
                small[a][b] = small[a][b] * root
            for a in range(b + 1, FEW):
                for c in range(b + 1, a + 1):
                    small[a][c] = small[a][c] - small[a][b] * small[c][b]
            column, up = raw[b], lines[b]
            for c in range(b):
                column = column - columns[c] * small[b][c]
                up = up - ups[c] * small[b][c]
            columns.append(column * root)
            ups.append(up * root)
        change = columns[0] * ups[0]
        for b in range(1, FEW):
            change = change + columns[b] * ups[b]
        value = jnp.where(row >= start + FEW, value - change, value)
        for b in range(FEW):
            value = jnp.where(row == start + b, ups[b], value)
    return value


def factor_kernel(scale, place_ref, gram_ref, *refs):
    *slices, factor_ref, ortho_ref, work = refs
    row = lax.broadcasted_iota(jnp.int32, (K, K), 0)
    lane = lax.broadcasted_iota(jnp.int32, (K, K), 1)
    work[:, :K] = gram_ref[...]
    work[:, K:] = (row == lane).astype(jnp.float32)
    small_row = lax.broadcasted_iota(jnp.int32, (BLOCK, K), 0)
    small_lane = lax.broadcasted_iota(jnp.int32, (BLOCK, K), 1)
    unit = (small_row + BLOCK == small_lane).astype(jnp.float32)
    for start in range(0, K, BLOCK):
        rows = slice(start, start + BLOCK)
        diagonal = work[rows, :K]
        if start:
            diagonal = pltpu.roll(diagonal, K - start, 1)
        done = eliminate(jnp.where(small_lane < BLOCK, diagonal, unit), BLOCK)
        inverse = pltpu.roll(done, K - BLOCK, 1)[:, :BLOCK]
        ups = dot_n(inverse, work[rows, :])
        work[rows, :] = ups
        below = start + BLOCK
        if below < K:
            change = dot_n(ups[:, :K].T, ups)
            work[below:, :] = work[below:, :] - change[below:]
    factor_ref[...] = (jnp.where(lane >= row, work[:, :K], 0.0) / scale).T
    own = place_ref[0]
    count = K // 4
    inverse = work[pl.ds(pl.multiple_of(own * count, count), count), K:] * scale
    inverse_high, inverse_low = split_bf16(inverse)
    both = jnp.concatenate([inverse_high, inverse_low], axis=0)
    width = 4 * BS
    mine, second, pair = slices
    for other, value in (
        (0, mine[...]),
        (2, second[...]),
        (1, pair[:K]),
        (3, pair[K:]),
    ):
        start = pl.multiple_of((own ^ other) * width, width)
        high, low = split_bf16(value)
        wide = dot_b(both, high)
        product = wide[:count] + (wide[count:] + dot_b(inverse_high, low))
        ortho_ref[:, pl.ds(start, width)] = product


def exchange(value, axis):
    return lax.ppermute(value, axis, [(0, 1), (1, 0)])


def to_all(value, axis):
    return lax.all_to_all(value, axis, 0, 0, tiled=True)


def filtered_basis(start_panel, tile_values, tile_rows, tile_cols, tile_counts):
    q = lax.axis_index("q")
    count_q = lax.axis_size("q")
    xh = lax.axis_index("xh")
    core = lax.axis_index("core")
    c = lax.axis_index("xl") * 2 + core
    quarter = TILE_CAP // 4

    even = [(i, i ^ 1) for i in range(count_q)]
    odd = [(i, (i + 1 if i % 2 else i - 1) % count_q) for i in range(count_q)]

    def halo(value):
        one = lax.ppermute(value, "q", even)
        two = lax.ppermute(value, "q", odd)
        return one, two

    count = 2 * count_q
    near = [(b, (b + 1 if b % 2 else b - 1) % count) for b in range(count)]
    diagonal = lax.ppermute(start_panel, ("q", "xh"), near)
    across = exchange(start_panel, "xh")
    one, two = halo(start_panel)
    ids = jnp.stack([q, xh, c])
    order = jax.ShapeDtypeStruct((2 * TILE_CAP + 3,), jnp.int32)
    split = jax.ShapeDtypeStruct((TILE_CAP, 2, BS, BS), jnp.bfloat16)
    own_tiles, own_list = pl.pallas_call(
        functools.partial(own_kernel, count_q),
        out_shape=(split, order),
        in_specs=[SMEM] * 4 + [pl.BlockSpec(memory_space=pltpu.MemorySpace.HBM)],
        out_specs=(VMEM, SMEM),
        scratch_shapes=[
            pltpu.VMEM((TILE_CAP, BS, BS), jnp.float32),
            pltpu.SemaphoreType.DMA((CHUNKS,)),
        ],
        compiler_params=pltpu.CompilerParams(vmem_limit_bytes=24 << 20),
        cost_estimate=pl.CostEstimate(flops=0, bytes_accessed=6 << 20, transcendentals=0),
        interpret=INTERPRET,
        name="own",
    )(ids, in_hbm(tile_rows), in_hbm(tile_cols), tile_counts, in_hbm(tile_values))
    piece = pl.pallas_call(
        cut_kernel,
        out_shape=jax.ShapeDtypeStruct((quarter + 1, BS, BS), jnp.float32),
        in_specs=[SMEM] * 2 + [VMEM] * 2 + [pl.BlockSpec(memory_space=pltpu.MemorySpace.HBM)],
        out_specs=VMEM,
        scratch_shapes=[pltpu.SemaphoreType.DMA],
        compiler_params=pltpu.CompilerParams(vmem_limit_bytes=24 << 20),
        interpret=INTERPRET,
        name="cut",
    )(ids, tile_counts, in_hbm(tile_rows[None]), in_hbm(tile_cols[None]), in_hbm(tile_values))
    first = lax.ppermute(piece, ("xh", "xl"), [(i, 3 - i) for i in range(4)])
    second = exchange(first, "xl")
    pair = jnp.concatenate([first, second], axis=0)
    far = exchange(pair, "core")
    half = jax.ShapeDtypeStruct((RB_DEV, COLS, BS), jnp.float32)
    mine, given, previous = call(
        functools.partial(first_kernel, count),
        (
            half,
            half,
            jax.ShapeDtypeStruct((HALF, COLS, BS), jnp.float32),
        ),
        [
            ids, tile_rows, tile_cols, tile_counts,
            start_panel, one, two, across, diagonal, own_tiles,
        ],
        [SMEM] * 4 + [VMEM] * 6,
        scratch=[
            pltpu.VMEM((5 * RB_DEV, 4 * COLS, BS), jnp.bfloat16),
            pltpu.VMEM((RB_DEV, 2 * COLS, BS), jnp.float32),
        ],
        flops=2 * TILE_CAP * 6 * COLS * BS * BS,
        moved=4 << 20,
    )
    got = exchange(given, "xh")
    current = jnp.concatenate([mine, got], axis=0)
    other_list = pl.pallas_call(
        functools.partial(partner_kernel, count_q),
        out_shape=order,
        in_specs=[SMEM, VMEM],
        out_specs=SMEM,
        scratch_shapes=[pltpu.SMEM((8, BS), jnp.float32), pltpu.SemaphoreType.DMA],
        compiler_params=pltpu.CompilerParams(vmem_limit_bytes=24 << 20),
        interpret=INTERPRET,
        name="partner",
    )(ids, first)
    other_tiles = call(other_kernel, split, [pair, far], [VMEM] * 2, moved=6 << 20)
    lists = (own_list, other_list)
    for step in range(1, DEGREE):
        even_half, odd_half = halo(current)
        tiles = (own_tiles, other_tiles, step == DEGREE - 1)
        part = graph_part(lists, (current,), (), *tiles)
        upcoming = graph_part(lists, (odd_half, even_half), (part, previous), *tiles)
        previous, current = current, upcoming

    parts = to_all(current.reshape(8, 4, COLS, BS), GROUP)
    everything, gram = call(
        gram_kernel,
        (
            jax.ShapeDtypeStruct((K, 4 * BS), jnp.float32),
            jax.ShapeDtypeStruct((K, K), jnp.float32),
        ),
        [parts],
        [VMEM],
        flops=2 * K * K * 4 * BS * 6,
        moved=1 << 20,
    )
    second = exchange(everything, "xl")
    far_slices = exchange(jnp.concatenate([everything, second], axis=0), "core")
    rows = K // count_q if K >= count_q else 1
    spread = to_all(gram, "q").reshape(count_q, rows, K).sum(axis=0)
    spread = to_all(jnp.broadcast_to(spread[None], (8, rows, K)), GROUP).sum(axis=0)
    gram = to_all(jnp.broadcast_to(spread[None], (count_q, rows, K)), "q").reshape(K, K)

    total_rows = start_panel.shape[1] * count_q * 2
    factor, ortho_panel = call(
        functools.partial(factor_kernel, math.sqrt(total_rows)),
        (
            jax.ShapeDtypeStruct((K, K), jnp.float32),
            jax.ShapeDtypeStruct((K // 4, 16 * BS), jnp.float32),
        ),
        [c[None], gram, everything, second, far_slices],
        [SMEM] + [VMEM] * 4,
        scratch=[pltpu.VMEM((K, 2 * K), jnp.float32)],
        flops=2 * K * K * 4 * BS * 6,
        moved=1 << 20,
    )
    return (ortho_panel, factor)


def solution(mesh):
    grid = Mesh(
        mesh.devices.reshape(mesh.devices.shape[0] // 2, 2, 2, 2), ("q", "xh", "xl", "core")
    )
    blk = ("q", "xh")
    in_specs = (P(COL, blk), P(blk, None, None), P(blk), P(blk), P(blk))
    out_specs = (P(COL, blk), P())
    return jax.shard_map(
        filtered_basis, mesh=grid, in_specs=in_specs, out_specs=out_specs, check_vma=False
    )
```
